32 devices in a mesh: grp: 2 (over core), own: 16 (over z, y, x).
Axes of the slice: x: 2, y: 2, z: 4, core: 2. Of those that a mesh axis runs over, the one named last changes fastest.
Arguments:
- activations: bfloat16 [8192, 1280], P(('grp', 'own')), may hold values from -18 to 18
- cotangents: bfloat16 [8192, 256], P(('grp', 'own')), may hold values from -18 to 18
- input_factor: float32 [2, 640, 640], P(None, 'grp'), may hold values from -0.4 to 3.6, as said below
- output_factor: float32 [256, 256], replicated, may hold values from -0.4 to 3.6, as said below
- gradient: float32 [2, 640, 256], P(None, 'grp'), may hold values from -4100 to 4100
- weights: float32 [2, 640, 256], P(None, 'grp'), may hold values from -6 to 6
- momentum: float32 [2, 640, 256], P(None, 'grp'), may hold values from -6 to 6
Outputs:
- new_weights: float32 [2, 640, 256], P(None, 'grp')
- new_momentum: float32 [2, 640, 256], P(None, 'grp')
- new_input: float32 [2, 640, 640], P(None, 'grp')
- new_output: float32 [256, 256], replicated
The draws below stay inside these ranges and needn't reach their ends.
Inputs may be any that keep to these rules, and one draw needn't show every extreme that they name: `input_factor`: each block is symmetric positive definite. `output_factor`: symmetric positive definite.
All inputs are finite; a program needn't handle non-finite values.
Results may differ from the reference program's by a relative error of at most 0.0003.
Values sent between devices are 32-bit elements; how exact they have to be, the bound alone decides.
No kernel may reach another device: no remote copies, remote signals or barrier semaphores. Data moves between devices by JAX's collectives and lax.ppermute only.
A program may use at most 64 MiB of HBM per device.

```python
import math
import jax
import jax.numpy as jnp
from jax import lax

DW = 1280
BLK = 640
RK = 256
ITERS = 3
NBLK = 2
TOKENS = 8192


shared_factors = 16


factor_weight = 0.3375


gradient_scale = 250.0


gradient_noise = 17.0


def layout(key, width, order):
    count = width // order
    keys = jax.random.split(jax.random.fold_in(key, 5), count)
    perms = jax.vmap(lambda single: jax.random.permutation(single, order))(keys)
    cluster = (perms.reshape(width) % shared_factors).astype(jnp.int32)
    loads = jnp.exp(jax.random.uniform(jax.random.fold_in(key, 7), (width,), minval=math.log(0.5), maxval=math.log(2.0)))
    return (cluster, loads)


def scaled_rows(key, count, cluster, loads):
    width = cluster.shape[0]
    column_scale = jnp.exp(jax.random.uniform(jax.random.fold_in(key, 2), (1, width), minval=math.log(0.3), maxval=math.log(3.0)))
    token_scale = jnp.exp(jax.random.uniform(jax.random.fold_in(key, 1), (count, 1), minval=math.log(0.5), maxval=math.log(2.0)))
    factors = jax.random.truncated_normal(jax.random.fold_in(key, 4), -4.0, 4.0, (count, shared_factors))
    noise = jax.random.truncated_normal(jax.random.fold_in(key, 3), -4.0, 4.0, (count, width))
    mixed = noise + 0.5 * jnp.roll(noise, 1, axis=1)
    loaded = jnp.take(factors, cluster, axis=1) * loads[None, :]
    values = token_scale * (0.5 * loaded + 0.3 * column_scale * mixed)
    return jnp.clip(values, -18.0, 18.0)


def band_matrix(key, order):
    diagonal = jnp.exp(jax.random.uniform(jax.random.fold_in(key, 1), (order,), minval=math.log(0.1), maxval=math.log(1.0)))
    rows = jax.lax.broadcasted_iota(jnp.int32, (order, order), 0)
    cols = jax.lax.broadcasted_iota(jnp.int32, (order, order), 1)
    matrix = jnp.where(rows == cols, diagonal[:, None], 0.0)
    for offset in (1, 2):
        values = jax.random.uniform(jax.random.fold_in(key, 10 + offset), (order,), minval=-1.0, maxval=1.0)
        near = 0.2 * jnp.minimum(diagonal, jnp.roll(diagonal, -offset)) * values
        matrix = matrix + jnp.where(cols == rows + offset, near[:, None], 0.0)
        matrix = matrix + jnp.where(rows == cols + offset, near[None, :], 0.0)
    return matrix


def factor_matrix(key, cluster, loads):
    order = cluster.shape[0]
    strength = jax.random.uniform(jax.random.fold_in(key, 20), (shared_factors,), minval=0.85, maxval=1.15)
    same = (cluster[:, None] == cluster[None, :]).astype(jnp.float32)
    row_strength = jnp.take(strength, cluster)
    lowrank = factor_weight * row_strength[:, None] * loads[:, None] * loads[None, :] * same
    return band_matrix(key, order) + lowrank


def draw_activations(key, part):
    cluster, loads = layout(jax.random.fold_in(key, 51), DW, BLK)
    return scaled_rows(jax.random.fold_in(key, 31), TOKENS, cluster, loads).astype(jnp.bfloat16)


def draw_cotangents(key, part):
    cluster, loads = layout(jax.random.fold_in(key, 52), RK, RK)
    return scaled_rows(jax.random.fold_in(key, 32), TOKENS, cluster, loads).astype(jnp.bfloat16)


def draw_input_factor(key, part):
    cluster, loads = layout(jax.random.fold_in(key, 51), DW, BLK)
    keys = jax.random.split(jax.random.fold_in(key, 41), NBLK)
    clusters = cluster.reshape(NBLK, BLK)
    block_loads = loads.reshape(NBLK, BLK)
    return jax.vmap(factor_matrix)(keys, clusters, block_loads).astype(jnp.float32)


def draw_output_factor(key, part):
    cluster, loads = layout(jax.random.fold_in(key, 52), RK, RK)
    return factor_matrix(jax.random.fold_in(key, 42), cluster, loads).astype(jnp.float32)


def draw_gradient(key, part):
    cluster_in, loads_in = layout(jax.random.fold_in(key, 51), DW, BLK)
    cluster_out, loads_out = layout(jax.random.fold_in(key, 52), RK, RK)
    tables = jax.random.truncated_normal(jax.random.fold_in(key, 61), -4.0, 4.0, (NBLK, shared_factors, shared_factors))
    noise = jax.random.truncated_normal(jax.random.fold_in(key, 62), -4.0, 4.0, (NBLK, BLK, RK))
    rows_cluster = cluster_in.reshape(NBLK, BLK)
    rows_loads = loads_in.reshape(NBLK, BLK)

    def one_block(table, row_cluster, row_loads):
        picked = jnp.take(jnp.take(table, row_cluster, axis=0), cluster_out, axis=1)
        return picked * row_loads[:, None] * loads_out[None, :]
    lowrank = jax.vmap(one_block)(tables, rows_cluster, rows_loads)
    return (gradient_scale * lowrank + gradient_noise * noise).astype(jnp.float32)


def block_levels(own_key, dims, shards, smallest, top_value):
    loudness, own = 1.0, jax.random.fold_in(own_key, 6)
    for dim, parts in shards:
        draws = jnp.exp(jax.random.uniform(jax.random.fold_in(own, dim), (parts,), jnp.float32, smallest / len(shards), top_value / len(shards)))
        loudness = loudness * jnp.repeat(draws, dims[dim] // parts).reshape([-1 if axis == dim else 1 for axis in range(len(dims))])
    return loudness


def scatter_about(rng, dims, spread, most, shards=(), held_as=jnp.bfloat16):
    factor_of = block_levels(rng, dims, shards, -0.22, 0.18) if shards else 1.0
    values = jax.random.normal(rng, dims, jnp.float32) * spread * factor_of
    return jnp.minimum(jnp.maximum(values, -most), most).astype(held_as)


def setup_inputs(seed: int = 0) -> dict:
    arg_keys = jax.random.split(jax.random.key(seed), 8)
    activations = draw_activations(jax.random.fold_in(arg_keys[7], 71), 0)
    cotangents = draw_cotangents(jax.random.fold_in(arg_keys[7], 71), 0)
    input_factor = draw_input_factor(jax.random.fold_in(arg_keys[7], 71), 0)
    output_factor = draw_output_factor(jax.random.fold_in(arg_keys[7], 71), 0)
    gradient = draw_gradient(jax.random.fold_in(arg_keys[7], 71), 0)
    weights = scatter_about(arg_keys[5], (NBLK, BLK, RK), 1.0, 6.0, ((1, 2),), jnp.float32)
    momentum = scatter_about(arg_keys[6], (NBLK, BLK, RK), 1.0, 6.0, ((1, 2),), jnp.float32)
    return dict(activations=activations, cotangents=cotangents, input_factor=input_factor, output_factor=output_factor, gradient=gradient, weights=weights, momentum=momentum)


damping = 0.1
mom_decay = 0.9
step_size = 0.5

def newton_start(damped, ident):
    squares = lax.optimization_barrier(jnp.sum(damped * damped, axis=(-2, -1), keepdims=True))
    bound = jnp.sqrt(squares)
    return 2.0 / bound * ident - damped / (bound * bound)

def newton_turn(damped, iterate):
    product = jnp.matmul(damped, iterate, precision=lax.Precision.HIGHEST)
    return 2.0 * iterate - jnp.matmul(product, iterate, precision=lax.Precision.HIGHEST)

def reference(activations, cotangents, input_factor, output_factor, gradient, weights, momentum):
    blocks = []
    for index in range(NBLK):
        piece = activations[:, index * BLK:(index + 1) * BLK]
        blocks.append(jnp.dot(piece.T, piece, preferred_element_type=jnp.float32))
    stat_in = jnp.stack(blocks)
    stat_out = jnp.dot(cotangents.T, cotangents, preferred_element_type=jnp.float32)
    new_input = 0.5 * input_factor + 0.5 * (stat_in / TOKENS)
    new_output = 0.5 * output_factor + 0.5 * (stat_out / TOKENS)
    ident_in = jnp.eye(BLK, dtype=jnp.float32)
    ident_out = jnp.eye(RK, dtype=jnp.float32)
    damped_in = new_input + damping * ident_in
    damped_out = new_output + damping * ident_out
    inverse_in = newton_start(damped_in, ident_in)
    inverse_out = newton_start(damped_out, ident_out)
    for iteration in range(ITERS - 1):
        inverse_in = newton_turn(damped_in, inverse_in)
        inverse_out = newton_turn(damped_out, inverse_out)
    precond = jnp.einsum('kij,kjr->kir', inverse_in, gradient, precision=lax.Precision.HIGHEST)
    update = jnp.einsum('kir,rs->kis', precond, inverse_out, precision=lax.Precision.HIGHEST)
    new_momentum = mom_decay * momentum + update
    new_weights = weights - step_size * new_momentum
    return (new_weights, new_momentum, new_input, new_output)
```

```python
import jax
import jax.numpy as jnp
from jax import lax
from jax.experimental import pallas as pl
from jax.experimental.pallas import tpu as pltpu
from jax.sharding import PartitionSpec as P

ITERS = 3


damping = 0.1
mom_decay = 0.9
step_size = 0.5

LANES = 128
SUBS = 8
SHARDS = 16


def newton_start(damped, ident):
    squares = jnp.sum(damped * damped, axis=(-2, -1), keepdims=True)
    bound = jnp.sqrt(squares)
    return 2.0 / bound * ident - damped / (bound * bound)


def step_rows(damped_rows, own_rows, full_iterate):
    product = jnp.matmul(damped_rows, full_iterate, precision=lax.Precision.HIGHEST)
    return 2.0 * own_rows - jnp.matmul(product, full_iterate, precision=lax.Precision.HIGHEST)


def any_mesh(activations, cotangents, input_factor, output_factor, gradient, weights, momentum):
    nblocks, slab, order = input_factor.shape
    rank = output_factor.shape[0]
    tokens = activations.shape[0]
    groups = lax.axis_size("grp")
    samples = tokens * groups * lax.axis_size("own")
    first_row = lax.axis_index("grp") * slab
    split_in = activations.reshape(tokens, nblocks, order)
    stat_in = jnp.einsum("tki,tkj->kij", split_in, split_in, preferred_element_type=jnp.float32)
    stat_out = jnp.einsum("ti,tj->ij", cotangents, cotangents, preferred_element_type=jnp.float32)
    total_in, total_out = lax.psum((stat_in, stat_out), ("grp", "own"))
    share_in = lax.dynamic_slice_in_dim(total_in, first_row, slab, 1)
    new_input = 0.5 * input_factor + 0.5 * (share_in / samples)
    new_output = 0.5 * output_factor + 0.5 * (total_out / samples)
    rows_in = lax.broadcasted_iota(jnp.int32, (slab, order), 0) + first_row
    cols_in = lax.broadcasted_iota(jnp.int32, (slab, order), 1)
    ident_rows = (rows_in == cols_in).astype(jnp.float32)
    ident_out = jnp.eye(rank, dtype=jnp.float32)
    damped_in = new_input + damping * ident_rows
    damped_out = new_output + damping * ident_out
    squares = lax.psum(jnp.sum(damped_in * damped_in, axis=(1, 2), keepdims=True), "grp")
    bound = jnp.sqrt(squares)
    iterate_in = 2.0 / bound * ident_rows - damped_in / (bound * bound)
    start_out = newton_start(damped_out, ident_out)
    out_rows = rank // groups
    first_out = lax.axis_index("grp") * out_rows
    damped_rows = lax.dynamic_slice_in_dim(damped_out, first_out, out_rows, 0)
    iterate_out = lax.dynamic_slice_in_dim(start_out, first_out, out_rows, 0)
    for iteration in range(ITERS - 1):
        full_in, full_out = (
            lax.all_gather(iterate_in, "grp", axis=1, tiled=True),
            lax.all_gather(iterate_out, "grp", axis=0, tiled=True),
        )
        iterate_in = step_rows(damped_in, iterate_in, full_in)
        iterate_out = step_rows(damped_rows, iterate_out, full_out)
    inverse_out = lax.all_gather(iterate_out, "grp", axis=0, tiled=True)
    precond = jnp.einsum(
        "kij,kjr->kir",
        iterate_in,
        lax.all_gather(gradient, "grp", axis=1, tiled=True),
        precision=lax.Precision.HIGHEST,
    )
    update = jnp.einsum("kir,rs->kis", precond, inverse_out, precision=lax.Precision.HIGHEST)
    new_momentum = mom_decay * momentum + update
    new_weights = weights - step_size * new_momentum
    return (new_weights, new_momentum, new_input, new_output)


def split(value):
    high = value.astype(jnp.bfloat16)
    low = (value - high.astype(jnp.float32)).astype(jnp.bfloat16)
    return high, low


def mul(a, b):
    return jnp.dot(a, b, preferred_element_type=jnp.float32)


def mul3(a, b):
    return mul(a[0], b[0]) + (mul(a[0], b[1]) + mul(a[1], b[0]))


def tile_pairs(tiles):
    return [(i, j) for i in range(tiles) for j in range(i, tiles)]


def stats_kernel(where_ref, act_ref, cot_ref, packed_ref):
    block, me = where_ref[0], where_ref[1]
    rank = cot_ref.shape[1]
    share = rank // 2
    order = act_ref.shape[1] // 2
    tiles = order // LANES
    places = [jnp.bitwise_xor(me, s) for s in range(SHARDS)]

    def put(index, tile):
        for s in range(SHARDS):
            packed_ref[places[s], index] = tile[s * SUBS : (s + 1) * SUBS]

    act = act_ref[:, pl.ds(pl.multiple_of(block * order, LANES), order)]
    turned = act.T
    index = 0
    for i in range(tiles):
        strip = mul(turned[i * LANES : (i + 1) * LANES], act[:, i * LANES :])
        for j in range(tiles - i):
            put(index, strip[:, j * LANES : (j + 1) * LANES])
            index += 1
    cot = cot_ref[:, pl.ds(pl.multiple_of(block * share, LANES), share)]
    strip = mul(cot.T, cot_ref[...])
    for i in range(share // LANES):
        for j in range(rank // LANES):
            put(index, strip[i * LANES : (i + 1) * LANES, j * LANES : (j + 1) * LANES])
            index += 1


def input_kernel(where_ref, near_ref, far_ref, fac_ref, fac_far_ref, grad_ref, grad_far_ref,
                 mine_ref, theirs_ref, left_ref, out_ref, stat_ref, fac_scr, grad_scr, *, scale):
    block, me = where_ref[0], where_ref[1]
    slab, order = fac_far_ref.shape
    tiles = order // LANES
    own_rows = pl.ds(pl.multiple_of(block * slab, SUBS), slab)
    far_rows = pl.ds(pl.multiple_of((1 - block) * slab, SUBS), slab)
    for place in range(SHARDS):
        rows = pl.ds(pl.multiple_of(jnp.bitwise_xor(me, place) * SUBS, SUBS), SUBS)
        half = SHARDS // 2
        stat_ref[:, rows, :] = near_ref[place] if place < half else far_ref[place - half]
    fac_scr[own_rows, :] = 0.5 * fac_ref[block]
    fac_scr[far_rows, :] = 0.5 * fac_far_ref[...]
    grad_scr[own_rows, :] = grad_ref[block]
    grad_scr[far_rows, :] = grad_far_ref[...]
    pairs = tile_pairs(tiles)
    for index, (i, j) in enumerate(pairs):
        at = lambda n: slice(n * LANES, (n + 1) * LANES)
        part = 0.5 * (stat_ref[index] * scale)
        fac_scr[at(i), at(j)] += part
        if i != j:
            fac_scr[at(j), at(i)] += part.T
    mine_ref[...] = fac_scr[own_rows, :]
    theirs_ref[...] = fac_scr[far_rows, :]
    lead = out_ref.shape[0] // LANES
    count = out_ref.shape[1] // LANES
    for n in range(lead * count):
        i, j = n // count, n % count
        out_ref[i * LANES : (i + 1) * LANES, j * LANES : (j + 1) * LANES] = stat_ref[len(pairs) + n]
    rows = lax.broadcasted_iota(jnp.int32, (order, order), 0)
    cols = lax.broadcasted_iota(jnp.int32, (order, order), 1)
    damped = fac_scr[...] + jnp.where(rows == cols, damping, 0.0)
    squares = jnp.sum(jnp.sum(damped * damped, axis=0, keepdims=True), axis=1, keepdims=True)
    over = 1.0 / jnp.sqrt(squares)
    scaled = damped * over
    first = split(scaled)
    twice = split(2.0 * scaled - mul3(first, first))
    grad = grad_scr[...]
    grad = 2.0 * grad - mul3(first, split(grad))
    grad = 2.0 * grad - mul3(twice, split(grad))
    once = grad - mul3(twice, split(grad))
    left_ref[...] = (grad + once - mul3(twice, split(once))) * over


def output_kernel(where_ref, stat_ref, stat_far_ref, fac_ref, left_ref, new_ref, mine_ref, theirs_ref, *, scale):
    block = where_ref[0]
    share, rank = stat_ref.shape
    slab = mine_ref.shape[0]
    own = pl.ds(pl.multiple_of(block * share, SUBS), share)
    far = pl.ds(pl.multiple_of((1 - block) * share, SUBS), share)
    new_ref[own, :] = 0.5 * fac_ref[own, :] + 0.5 * (stat_ref[...] * scale)
    new_ref[far, :] = 0.5 * fac_ref[far, :] + 0.5 * (stat_far_ref[...] * scale)
    rows = lax.broadcasted_iota(jnp.int32, (rank, rank), 0)
    cols = lax.broadcasted_iota(jnp.int32, (rank, rank), 1)
    damped = new_ref[...] + jnp.where(rows == cols, damping, 0.0)
    squares = jnp.sum(jnp.sum(damped * damped, axis=0, keepdims=True), axis=1, keepdims=True)
    over = 1.0 / jnp.sqrt(squares)
    scaled = damped * over
    first = split(scaled)
    twice = 2.0 * scaled - mul3(first, first)
    second = split(twice)
    fourth = split(2.0 * twice - mul3(second, second))
    head = jnp.where(rows == cols, 4.0, 0.0) - 2.0 * (scaled + twice) + mul3(first, second)
    inverse = split((2.0 * head - mul3(split(head), fourth)) * over)
    far_left = split(left_ref[pl.ds(pl.multiple_of((1 - block) * slab, SUBS), slab), :])
    theirs_ref[...] = mul3(far_left, inverse)
    own_left = split(left_ref[pl.ds(pl.multiple_of(block * slab, SUBS), slab), :])
    mine_ref[...] = mul3(own_left, inverse)


def call(kernel, where, args, outs, scratch=()):
    return pl.pallas_call(
        kernel,
        out_shape=[jax.ShapeDtypeStruct(shape, jnp.float32) for shape in outs],
        in_specs=[pl.BlockSpec(memory_space=pltpu.SMEM)]
        + [pl.BlockSpec(memory_space=pltpu.VMEM)] * len(args),
        out_specs=[pl.BlockSpec(memory_space=pltpu.VMEM)] * len(outs),
        scratch_shapes=[pltpu.VMEM(shape, jnp.float32) for shape in scratch],
    )(where, *args)


def on_chip_pairs(activations, cotangents, input_factor, output_factor, gradient, weights, momentum):
    nblocks, slab, order = input_factor.shape
    rank = output_factor.shape[0]
    group = lax.axis_index("grp")
    spot = lax.axis_index("own")
    peers = lax.axis_size("own")
    samples = activations.shape[0] * lax.axis_size("grp") * peers
    scale = 1.0 / samples
    x_bit, y_bit, z_bits = spot % 2, (spot // 2) % 2, spot // 4
    straight = x_bit * 8 + y_bit * 4 + z_bits
    crossed = y_bit * 8 + x_bit * 4 + z_bits
    me = jnp.where(group == 0, straight, crossed)
    partner = jnp.where(group == 0, crossed, straight)
    where_mine = jnp.stack([group, me]).astype(jnp.int32)
    where_theirs = jnp.stack([1 - group, partner]).astype(jnp.int32)
    ntiles = len(tile_pairs(order // LANES)) + (rank // 2 // LANES) * (rank // LANES)
    packed = (SHARDS, ntiles, SUBS, LANES)

    def swap(value):
        return lax.ppermute(value, "grp", [(0, 1), (1, 0)])

    def send(value, flips):
        pairs = [(g * peers + o, g * peers + (o ^ flips[g])) for g in range(2) for o in range(peers)]
        return lax.ppermute(value, ("grp", "own"), pairs)

    (theirs,) = call(stats_kernel, where_theirs, (activations, cotangents), [packed])
    arrived = swap(theirs)
    (held,) = call(stats_kernel, where_mine, (activations, cotangents), [packed])
    fac_far = swap(lax.dynamic_index_in_dim(input_factor, 1 - group, 0, False))
    grad_far = swap(lax.dynamic_index_in_dim(gradient, 1 - group, 0, False))

    arrived = send(held[8:] + arrived[8:], (1, 2)), held[:8] + arrived[:8]
    low = send(arrived[0][4:] + arrived[1][4:], (2, 1)), arrived[0][:4] + arrived[1][:4]
    quarter = low[0] + low[1]
    pieces = [send(quarter[d : d + 1], (4 * d, 4 * d)) for d in (3, 2, 1)]
    total = quarter[:1] + pieces[0] + pieces[1] + pieces[2]
    gathered = {d: send(total, (4 * d, 4 * d)) for d in (3, 2, 1)}
    quarter = jnp.concatenate([total, gathered[1], gathered[2], gathered[3]], 0)
    near = jnp.concatenate([quarter, send(quarter, (2, 1))], 0)
    far = send(near, (1, 2))

    mine, theirs, left, out_share = call(
        lambda *refs: input_kernel(*refs, scale=scale),
        where_mine,
        (near, far, input_factor, fac_far, gradient, grad_far),
        [(slab, order), (slab, order), (order, rank), (rank // 2, rank)],
        [(ntiles, LANES, LANES), (order, order), (order, rank)],
    )
    out_far = swap(out_share)
    rows_far = swap(theirs)
    new_output, update, update_far = call(
        lambda *refs: output_kernel(*refs, scale=scale),
        where_mine,
        (out_share, out_far, output_factor, left),
        [(rank, rank), (slab, rank), (slab, rank)],
    )
    update_far = swap(update_far)
    own_block = lax.broadcasted_iota(jnp.int32, (nblocks, 1, 1), 0) == group
    new_input = jnp.where(own_block, mine[None], rows_far[None])
    new_momentum = mom_decay * momentum + jnp.where(own_block, update[None], update_far[None])
    new_weights = weights - step_size * new_momentum
    return (new_weights, new_momentum, new_input, new_output)


def solution(mesh):
    placed = (
        P(("grp", "own"), None),
        P(("grp", "own"), None),
        P(None, "grp", None),
        P(),
        P(None, "grp", None),
        P(None, "grp", None),
        P(None, "grp", None),
    )

    def on_device(*args):
        nblocks, slab, order = args[2].shape
        rank = args[3].shape[0]
        fits = nblocks == 2 and order % LANES == 0 and slab % SUBS == 0 and rank % (2 * LANES) == 0
        paired = mesh.shape["grp"] == 2 and mesh.shape["own"] == SHARDS
        return (on_chip_pairs if fits and paired else any_mesh)(*args)

    return jax.shard_map(
        on_device,
        mesh=mesh,
        in_specs=placed,
        out_specs=(P(None, "grp", None), P(None, "grp", None), P(None, "grp", None), P()),
        check_vma=False,
    )
```

```python
import jax
import jax.numpy as jnp
from jax import lax
from jax.experimental import pallas as pl
from jax.experimental.pallas import tpu as pltpu
from jax.sharding import PartitionSpec as P

ITERS = 3


damping = 0.1
mom_decay = 0.9
step_size = 0.5

LANES = 128
SUBS = 8
SHARDS = 16


def newton_start(damped, ident):
    squares = jnp.sum(damped * damped, axis=(-2, -1), keepdims=True)
    bound = jnp.sqrt(squares)
    return 2.0 / bound * ident - damped / (bound * bound)


def step_rows(damped_rows, own_rows, full_iterate):
    product = jnp.matmul(damped_rows, full_iterate, precision=lax.Precision.HIGHEST)
    return 2.0 * own_rows - jnp.matmul(product, full_iterate, precision=lax.Precision.HIGHEST)


def any_mesh(activations, cotangents, input_factor, output_factor, gradient, weights, momentum):
    nblocks, slab, order = input_factor.shape
    rank = output_factor.shape[0]
    tokens = activations.shape[0]
    groups = lax.axis_size("grp")
    samples = tokens * groups * lax.axis_size("own")
    first_row = lax.axis_index("grp") * slab
    split_in = activations.reshape(tokens, nblocks, order)
    stat_in = jnp.einsum("tki,tkj->kij", split_in, split_in, preferred_element_type=jnp.float32)
    stat_out = jnp.einsum("ti,tj->ij", cotangents, cotangents, preferred_element_type=jnp.float32)
    total_in, total_out = lax.psum((stat_in, stat_out), ("grp", "own"))
    share_in = lax.dynamic_slice_in_dim(total_in, first_row, slab, 1)
    new_input = 0.5 * input_factor + 0.5 * (share_in / samples)
    new_output = 0.5 * output_factor + 0.5 * (total_out / samples)
    rows_in = lax.broadcasted_iota(jnp.int32, (slab, order), 0) + first_row
    cols_in = lax.broadcasted_iota(jnp.int32, (slab, order), 1)
    ident_rows = (rows_in == cols_in).astype(jnp.float32)
    ident_out = jnp.eye(rank, dtype=jnp.float32)
    damped_in = new_input + damping * ident_rows
    damped_out = new_output + damping * ident_out
    squares = lax.psum(jnp.sum(damped_in * damped_in, axis=(1, 2), keepdims=True), "grp")
    bound = jnp.sqrt(squares)
    iterate_in = 2.0 / bound * ident_rows - damped_in / (bound * bound)
    start_out = newton_start(damped_out, ident_out)
    out_rows = rank // groups
    first_out = lax.axis_index("grp") * out_rows
    damped_rows = lax.dynamic_slice_in_dim(damped_out, first_out, out_rows, 0)
    iterate_out = lax.dynamic_slice_in_dim(start_out, first_out, out_rows, 0)
    for iteration in range(ITERS - 1):
        full_in, full_out = (
            lax.all_gather(iterate_in, "grp", axis=1, tiled=True),
            lax.all_gather(iterate_out, "grp", axis=0, tiled=True),
        )
        iterate_in = step_rows(damped_in, iterate_in, full_in)
        iterate_out = step_rows(damped_rows, iterate_out, full_out)
    inverse_out = lax.all_gather(iterate_out, "grp", axis=0, tiled=True)
    precond = jnp.einsum(
        "kij,kjr->kir",
        iterate_in,
        lax.all_gather(gradient, "grp", axis=1, tiled=True),
        precision=lax.Precision.HIGHEST,
    )
    update = jnp.einsum("kir,rs->kis", precond, inverse_out, precision=lax.Precision.HIGHEST)
    new_momentum = mom_decay * momentum + update
    new_weights = weights - step_size * new_momentum
    return (new_weights, new_momentum, new_input, new_output)


def split(value):
    high = value.astype(jnp.bfloat16)
    low = (value - high.astype(jnp.float32)).astype(jnp.bfloat16)
    return high, low


def mul(a, b):
    return jnp.dot(a, b, preferred_element_type=jnp.float32)


def mul3(a, b):
    return mul(a[0], b[0]) + (mul(a[0], b[1]) + mul(a[1], b[0]))


def apply3(a, b):
    b = split(b)
    half = a[0].shape[0] // 2
    return jnp.concatenate([mul3([v[:half] for v in a], b), mul3([v[half:] for v in a], b)], 0)


def twice_less_square(value, halves):
    order = value.shape[0]
    ends = list(range(order, 0, -2 * LANES))[::-1]
    strips = []
    for end in ends:
        cols = slice(max(end - 2 * LANES, 0), end)
        square = mul3([v[:end] for v in halves], [v[:, cols] for v in halves])
        strips.append(split(2.0 * value[:end, cols] - square))
    parts = []
    for part in range(2):
        rows = []
        for n, end in enumerate(ends):
            top = ends[n - 1] if n else 0
            left = [strips[n][part][:top].T] if n else []
            right = [strips[m][part][top:end] for m in range(n, len(ends))]
            rows.append(jnp.concatenate(left + right, 1))
        parts.append(jnp.concatenate(rows, 0))
    return parts


def tile_pairs(tiles):
    return [(i, j) for i in range(tiles) for j in range(i, tiles)]


def stats_kernel(where_ref, act_ref, cot_ref, packed_ref, *, far):
    block = 1 - where_ref[0] if far else where_ref[0]
    me = where_ref[2] if far else where_ref[1]
    rank = cot_ref.shape[1]
    share = rank // 2
    order = act_ref.shape[1] // 2
    tiles = order // LANES
    places = [jnp.bitwise_xor(me, s) for s in range(SHARDS)]

    def put(index, tile):
        for s in range(SHARDS):
            packed_ref[places[s], index] = tile[s * SUBS : (s + 1) * SUBS]

    index = 0
    cot = cot_ref[:, pl.ds(pl.multiple_of(block * share, LANES), share)]
    strip = mul(cot.T, cot_ref[...])
    for i in range(share // LANES):
        for j in range(rank // LANES):
            put(index, strip[i * LANES : (i + 1) * LANES, j * LANES : (j + 1) * LANES])
            index += 1
    act = act_ref[:, pl.ds(pl.multiple_of(block * order, LANES), order)]
    turned = act.T
    for i in range(tiles):
        strip = mul(turned[i * LANES : (i + 1) * LANES], act[:, i * LANES :])
        for j in range(tiles - i):
            put(index, strip[:, j * LANES : (j + 1) * LANES])
            index += 1


def spread(me, halves, put):
    for place in range(SHARDS):
        half = halves[place * len(halves) // SHARDS]
        put(pl.multiple_of(jnp.bitwise_xor(me, place) * SUBS, SUBS), half[place % half.shape[0]])


def input_kernel(where_ref, near_ref, far_ref, fac_ref, fac_far_ref, grad_ref, grad_far_ref,
                 mine_ref, theirs_ref, left_ref, stat_ref, fac_scr, grad_scr, *, scale, skip):
    block, me = where_ref[0], where_ref[1]
    slab, order = fac_far_ref.shape
    tiles = order // LANES
    own_rows = pl.ds(pl.multiple_of(block * slab, SUBS), slab)
    far_rows = pl.ds(pl.multiple_of((1 - block) * slab, SUBS), slab)
    def put(row, rows):
        stat_ref[:, pl.ds(row, SUBS), :] = rows[skip:]

    spread(me, (near_ref, far_ref), put)
    fac_scr[own_rows, :] = 0.5 * fac_ref[block]
    fac_scr[far_rows, :] = 0.5 * fac_far_ref[...]
    grad_scr[own_rows, :] = grad_ref[block]
    grad_scr[far_rows, :] = grad_far_ref[...]
    for index, (i, j) in enumerate(tile_pairs(tiles)):
        at = lambda n: slice(n * LANES, (n + 1) * LANES)
        part = 0.5 * (stat_ref[index] * scale)
        fac_scr[at(i), at(j)] += part
        if i != j:
            fac_scr[at(j), at(i)] += part.T
    mine_ref[...] = fac_scr[own_rows, :]
    theirs_ref[...] = fac_scr[far_rows, :]
    rows = lax.broadcasted_iota(jnp.int32, (order, order), 0)
    cols = lax.broadcasted_iota(jnp.int32, (order, order), 1)
    damped = fac_scr[...] + jnp.where(rows == cols, damping, 0.0)
    squares = jnp.sum(jnp.sum(damped * damped, axis=0, keepdims=True), axis=1, keepdims=True)
    over = 1.0 / jnp.sqrt(squares)
    scaled = damped * over
    first = split(scaled)
    twice = twice_less_square(scaled, first)
    grad = grad_scr[...]
    grad = 2.0 * grad - apply3(first, grad)
    grad = 2.0 * grad - apply3(twice, grad)
    once = grad - apply3(twice, grad)
    left_ref[...] = (grad + once - apply3(twice, once)) * over


def output_kernel(where_ref, stat_ref, other_ref, fac_ref, left_ref, new_ref, mine_ref, theirs_ref, *, scale):
    block, me, other = where_ref[0], where_ref[1], where_ref[2]
    rank = fac_ref.shape[0]
    share = rank // 2
    count = rank // LANES

    def put(first):
        def rows_of(row, tiles):
            for n in range(share // LANES * count):
                i, j = n // count, n % count
                at = pl.ds(pl.multiple_of(first + i * LANES + row, SUBS), SUBS)
                cols = slice(j * LANES, (j + 1) * LANES)
                new_ref[at, cols] = 0.5 * fac_ref[at, cols] + 0.5 * (tiles[n] * scale)
        return rows_of

    spread(me, (stat_ref,), put(block * share))
    spread(other, (other_ref,), put((1 - block) * share))
    rows = lax.broadcasted_iota(jnp.int32, (rank, rank), 0)
    cols = lax.broadcasted_iota(jnp.int32, (rank, rank), 1)
    damped = new_ref[...] + jnp.where(rows == cols, damping, 0.0)
    squares = jnp.sum(jnp.sum(damped * damped, axis=0, keepdims=True), axis=1, keepdims=True)
    over = 1.0 / jnp.sqrt(squares)
    scaled = damped * over
    first = split(scaled)
    twice = 2.0 * scaled - mul3(first, first)
    second = split(twice)
    fourth = split(2.0 * twice - mul3(second, second))
    head = jnp.where(rows == cols, 4.0, 0.0) - 2.0 * (scaled + twice) + mul3(first, second)
    inverse = split((2.0 * head - mul3(split(head), fourth)) * over)
    slab = mine_ref.shape[0]
    theirs_ref[...] = mul3(split(left_ref[pl.ds(pl.multiple_of((1 - block) * slab, SUBS), slab), :]), inverse)
    mine_ref[...] = mul3(split(left_ref[pl.ds(pl.multiple_of(block * slab, SUBS), slab), :]), inverse)


def call(kernel, where, args, outs, scratch=()):
    return pl.pallas_call(
        kernel,
        out_shape=[jax.ShapeDtypeStruct(shape, jnp.float32) for shape in outs],
        in_specs=[pl.BlockSpec(memory_space=pltpu.SMEM)]
        + [pl.BlockSpec(memory_space=pltpu.VMEM)] * len(args),
        out_specs=[pl.BlockSpec(memory_space=pltpu.VMEM)] * len(outs),
        scratch_shapes=[pltpu.VMEM(shape, jnp.float32) for shape in scratch],
    )(where, *args)


def on_chip_pairs(activations, cotangents, input_factor, output_factor, gradient, weights, momentum):
    nblocks, slab, order = input_factor.shape
    rank = output_factor.shape[0]
    group = lax.axis_index("grp")
    spot = lax.axis_index("own")
    peers = lax.axis_size("own")
    samples = activations.shape[0] * lax.axis_size("grp") * peers
    scale = 1.0 / samples
    x_bit, y_bit, z_bits = spot % 2, (spot // 2) % 2, spot // 4
    straight = x_bit * 8 + y_bit * 4 + z_bits
    crossed = y_bit * 8 + x_bit * 4 + z_bits
    me = jnp.where(group == 0, straight, crossed)
    partner = jnp.where(group == 0, crossed, straight)
    where = jnp.stack([group, me, partner]).astype(jnp.int32)
    outs = (rank // 2 // LANES) * (rank // LANES)
    packed = [(SHARDS, outs + len(tile_pairs(order // LANES)), SUBS, LANES)]
    fence = lax.optimization_barrier

    def swap(value):
        return lax.ppermute(value, "grp", [(0, 1), (1, 0)])

    def send(value, flips):
        pairs = [(g * peers + o, g * peers + (o ^ flips[g])) for g in range(2) for o in range(peers)]
        return lax.ppermute(value, ("grp", "own"), pairs)

    def stats(far):
        return call(lambda *refs: stats_kernel(*refs, far=far), where, (activations, cotangents), packed)[0]

    arrived = swap(stats(True))
    held = stats(False)
    going = held[8:] + arrived[8:]
    came = send(going, (1, 2))
    fac_rows, grad_rows, _ = fence((input_factor, gradient, going))
    fac_far = swap(lax.dynamic_index_in_dim(fac_rows, 1 - group, 0, False))
    grad_far = swap(lax.dynamic_index_in_dim(grad_rows, 1 - group, 0, False))
    came, fac_far, grad_far = fence((came, fac_far, grad_far))
    kept = held[:8] + arrived[:8]
    came = send(kept[4:] + came[4:], (2, 1)), kept[:4] + came[:4]
    kept = came[0] + came[1]
    ways = (3, 2, 1)
    pieces = {d: send(kept[d : d + 1], (4 * d, 4 * d)) for d in ways}
    kept = kept[:1] + pieces[3] + pieces[2] + pieces[1]
    pieces = {d: send(kept, (4 * d, 4 * d)) for d in ways}
    kept = jnp.concatenate([kept, pieces[1], pieces[2], pieces[3]], 0)
    near = jnp.concatenate([kept, send(kept, (2, 1))], 0)
    far = send(near, (1, 2))

    share = jnp.concatenate([near[:, :outs], far[:, :outs]], 0)
    share_far = swap(share)
    mine, theirs, left = call(
        lambda *refs: input_kernel(*refs, scale=scale, skip=outs),
        where,
        (near, far, input_factor, fac_far, gradient, grad_far),
        [(slab, order), (slab, order), (order, rank)],
        [(packed[0][1] - outs, LANES, LANES), (order, order), (order, rank)],
    )
    new_output, update, update_far = call(
        lambda *refs: output_kernel(*refs, scale=scale),
        where,
        (share, share_far, output_factor, left),
        [(rank, rank), (slab, rank), (slab, rank)],
    )
    rows_far = swap(theirs)
    update_far = swap(update_far)
    own_block = lax.broadcasted_iota(jnp.int32, (nblocks, 1, 1), 0) == group
    new_input = jnp.where(own_block, mine[None], rows_far[None])
    update_far, _ = fence((update_far, new_input))
    new_momentum = mom_decay * momentum + jnp.where(own_block, update[None], update_far[None])
    new_weights = weights - step_size * new_momentum
    return (new_weights, new_momentum, new_input, new_output)


def solution(mesh):
    placed = (
        P(("grp", "own"), None),
        P(("grp", "own"), None),
        P(None, "grp", None),
        P(),
        P(None, "grp", None),
        P(None, "grp", None),
        P(None, "grp", None),
    )

    def on_device(*args):
        nblocks, slab, order = args[2].shape
        rank = args[3].shape[0]
        fits = nblocks == 2 and order % LANES == 0 and slab % SUBS == 0 and rank % (2 * LANES) == 0
        paired = mesh.shape["grp"] == 2 and mesh.shape["own"] == SHARDS
        return (on_chip_pairs if fits and paired else any_mesh)(*args)

    return jax.shard_map(
        on_device,
        mesh=mesh,
        in_specs=placed,
        out_specs=(P(None, "grp", None), P(None, "grp", None), P(None, "grp", None), P()),
        check_vma=False,
    )
```

```python
import math

import jax
import jax.numpy as jnp
from jax import lax
from jax.experimental import pallas as pl
from jax.experimental.pallas import tpu as pltpu
from jax.sharding import PartitionSpec as P

ITERS = 3


damping = 0.1
mom_decay = 0.9
step_size = 0.5

LANES = 128
SUBS = 8
SHARDS = 16


def newton_start(damped, ident):
    squares = jnp.sum(damped * damped, axis=(-2, -1), keepdims=True)
    bound = jnp.sqrt(squares)
    return 2.0 / bound * ident - damped / (bound * bound)


def step_rows(damped_rows, own_rows, full_iterate):
    product = jnp.matmul(damped_rows, full_iterate, precision=lax.Precision.HIGHEST)
    return 2.0 * own_rows - jnp.matmul(product, full_iterate, precision=lax.Precision.HIGHEST)


def any_mesh(activations, cotangents, input_factor, output_factor, gradient, weights, momentum):
    nblocks, slab, order = input_factor.shape
    rank = output_factor.shape[0]
    tokens = activations.shape[0]
    groups = lax.axis_size("grp")
    samples = tokens * groups * lax.axis_size("own")
    first_row = lax.axis_index("grp") * slab
    split_in = activations.reshape(tokens, nblocks, order)
    stat_in = jnp.einsum("tki,tkj->kij", split_in, split_in, preferred_element_type=jnp.float32)
    stat_out = jnp.einsum("ti,tj->ij", cotangents, cotangents, preferred_element_type=jnp.float32)
    total_in, total_out = lax.psum((stat_in, stat_out), ("grp", "own"))
    share_in = lax.dynamic_slice_in_dim(total_in, first_row, slab, 1)
    new_input = 0.5 * input_factor + 0.5 * (share_in / samples)
    new_output = 0.5 * output_factor + 0.5 * (total_out / samples)
    rows_in = lax.broadcasted_iota(jnp.int32, (slab, order), 0) + first_row
    cols_in = lax.broadcasted_iota(jnp.int32, (slab, order), 1)
    ident_rows = (rows_in == cols_in).astype(jnp.float32)
    ident_out = jnp.eye(rank, dtype=jnp.float32)
    damped_in = new_input + damping * ident_rows
    damped_out = new_output + damping * ident_out
    squares = lax.psum(jnp.sum(damped_in * damped_in, axis=(1, 2), keepdims=True), "grp")
    bound = jnp.sqrt(squares)
    iterate_in = 2.0 / bound * ident_rows - damped_in / (bound * bound)
    start_out = newton_start(damped_out, ident_out)
    out_rows = rank // groups
    first_out = lax.axis_index("grp") * out_rows
    damped_rows = lax.dynamic_slice_in_dim(damped_out, first_out, out_rows, 0)
    iterate_out = lax.dynamic_slice_in_dim(start_out, first_out, out_rows, 0)
    for iteration in range(ITERS - 1):
        full_in, full_out = (
            lax.all_gather(iterate_in, "grp", axis=1, tiled=True),
            lax.all_gather(iterate_out, "grp", axis=0, tiled=True),
        )
        iterate_in = step_rows(damped_in, iterate_in, full_in)
        iterate_out = step_rows(damped_rows, iterate_out, full_out)
    inverse_out = lax.all_gather(iterate_out, "grp", axis=0, tiled=True)
    precond = jnp.einsum(
        "kij,kjr->kir",
        iterate_in,
        lax.all_gather(gradient, "grp", axis=1, tiled=True),
        precision=lax.Precision.HIGHEST,
    )
    update = jnp.einsum("kir,rs->kis", precond, inverse_out, precision=lax.Precision.HIGHEST)
    new_momentum = mom_decay * momentum + update
    new_weights = weights - step_size * new_momentum
    return (new_weights, new_momentum, new_input, new_output)


def split(value):
    high = value.astype(jnp.bfloat16)
    low = (value - high.astype(jnp.float32)).astype(jnp.bfloat16)
    return high, low


def mul(a, b):
    return jnp.dot(a, b, preferred_element_type=jnp.float32)


def mul3(a, b):
    return mul(a[0], b[0]) + (mul(a[0], b[1]) + mul(a[1], b[0]))


def apply3(a, b):
    b = split(b)
    half = a[0].shape[0] // 2
    return jnp.concatenate([mul3([v[:half] for v in a], b), mul3([v[half:] for v in a], b)], 0)


def twice_less_square(value, halves):
    order = value.shape[0]
    ends = list(range(order, 0, -2 * LANES))[::-1]
    strips = []
    for end in ends:
        cols = slice(max(end - 2 * LANES, 0), end)
        square = mul3([v[:end] for v in halves], [v[:, cols] for v in halves])
        strips.append(split(2.0 * value[:end, cols] - square))
    parts = []
    for part in range(2):
        rows = []
        for n, end in enumerate(ends):
            top = ends[n - 1] if n else 0
            left = [strips[n][part][:top].T] if n else []
            right = [strips[m][part][top:end] for m in range(n, len(ends))]
            rows.append(jnp.concatenate(left + right, 1))
        parts.append(jnp.concatenate(rows, 0))
    return parts


def tile_pairs(tiles):
    return [(i, j) for i in range(tiles) for j in range(i, tiles)]


def places_in(shape):
    rows = lax.broadcasted_iota(jnp.int32, shape, 0)
    cols = lax.broadcasted_iota(jnp.int32, shape, 1)
    return rows, cols


def stats_kernel(where_ref, act_ref, cot_ref, packed_ref, *, far):
    block = 1 - where_ref[0] if far else where_ref[0]
    me = where_ref[2] if far else where_ref[1]
    order = act_ref.shape[1] // 2
    tiles = order // LANES
    places = [jnp.bitwise_xor(me, s) for s in range(SHARDS)]

    def put(index, tile):
        for s in range(SHARDS):
            packed_ref[places[s], index] = tile[s * SUBS : (s + 1) * SUBS]

    index = 2
    act = act_ref[:, pl.ds(pl.multiple_of(block * order, LANES), order)]
    turned = act.T
    diagonal = []
    for i in range(tiles):
        strip = mul(turned[i * LANES : (i + 1) * LANES], act[:, i * LANES :])
        diagonal.append(strip[:, :LANES])
        for j in range(1, tiles - i):
            put(index, strip[:, j * LANES : (j + 1) * LANES])
            index += 1
    cot = cot_ref[:, pl.ds(pl.multiple_of(block * LANES, LANES), LANES)]
    diagonal.append(mul(cot.T, cot))
    upper = mul(cot_ref[:, :LANES].T, cot_ref[:, LANES:])
    half = LANES // 2
    upper = jnp.where(block == 0, upper[:half], upper[half:])
    rows, cols = places_in((LANES, LANES))
    npairs = len(diagonal) // 2
    lines = []
    for pair in range(npairs):
        above, below = diagonal[2 * pair], diagonal[2 * pair + 1]
        put(index + pair if pair < npairs - 1 else 0, jnp.where(cols > rows, above, below))
        lines.append(jnp.sum(jnp.where(cols == rows, above, 0.0).reshape(SHARDS, SUBS, LANES), axis=1))
    few = SUBS // 2
    for s in range(SHARDS):
        packed_ref[places[s], 1, :few] = upper[s * few : (s + 1) * few]
        for pair in range(few):
            line = lines[pair][s : s + 1] if pair < npairs else jnp.zeros((1, LANES), jnp.float32)
            packed_ref[places[s], 1, few + pair : few + pair + 1] = line


def spread(me, halves, put):
    for place in range(SHARDS):
        half = halves[place * len(halves) // SHARDS]
        put(pl.multiple_of(jnp.bitwise_xor(me, place) * SUBS, SUBS), half[place % half.shape[0]])


def input_kernel(where_ref, near_ref, far_ref, fac_ref, fac_far_ref, grad_ref, grad_far_ref,
                 mine_ref, theirs_ref, left_ref, stat_ref, fac_scr, grad_scr, *, scale):
    block, me = where_ref[0], where_ref[1]
    slab, order = fac_far_ref.shape
    tiles = order // LANES
    own_rows = pl.ds(pl.multiple_of(block * slab, SUBS), slab)
    far_rows = pl.ds(pl.multiple_of((1 - block) * slab, SUBS), slab)
    def put(row, rows):
        stat_ref[:, pl.ds(row, SUBS), :] = rows

    spread(me, (near_ref, far_ref), put)
    fac_scr[own_rows, :] = 0.5 * fac_ref[block]
    fac_scr[far_rows, :] = 0.5 * fac_far_ref[...]
    grad_scr[own_rows, :] = grad_ref[block]
    grad_scr[far_rows, :] = grad_far_ref[...]
    at = lambda n: slice(n * LANES, (n + 1) * LANES)
    index = 2
    for i in range(tiles):
        for j in range(i + 1, tiles):
            part = 0.5 * (stat_ref[index] * scale)
            fac_scr[at(i), at(j)] += part
            fac_scr[at(j), at(i)] += part.T
            index += 1
    rows, cols = places_in((LANES, LANES))
    npairs = (tiles + 1) // 2
    for pair in range(npairs):
        part = 0.5 * (stat_ref[index + pair if pair < npairs - 1 else 0] * scale)
        turned = part.T
        line = stat_ref[1, pl.ds(SUBS // 2 + pair, SHARDS, stride=SUBS), :]
        line = 0.5 * (jnp.sum(line, axis=0, keepdims=True) * scale)
        above = jnp.where(cols > rows, part, jnp.where(cols < rows, turned, line))
        fac_scr[at(2 * pair), at(2 * pair)] += above
        if pair < npairs - 1:
            fac_scr[at(2 * pair + 1), at(2 * pair + 1)] += jnp.where(cols > rows, turned, part)
    mine_ref[...] = fac_scr[own_rows, :]
    theirs_ref[...] = fac_scr[far_rows, :]
    rows = lax.broadcasted_iota(jnp.int32, (order, order), 0)
    cols = lax.broadcasted_iota(jnp.int32, (order, order), 1)
    damped = fac_scr[...] + jnp.where(rows == cols, damping, 0.0)
    squares = jnp.sum(jnp.sum(damped * damped, axis=0, keepdims=True), axis=1, keepdims=True)
    over = 1.0 / jnp.sqrt(squares)
    scaled = damped * over
    first = split(scaled)
    twice = twice_less_square(scaled, first)
    grad = grad_scr[...]
    grad = 2.0 * grad - apply3(first, grad)
    grad = 2.0 * grad - apply3(twice, grad)
    once = grad - apply3(twice, grad)
    left_ref[...] = (grad + once - apply3(twice, once)) * over


def output_kernel(where_ref, near_ref, far_ref, other_near_ref, other_far_ref, fac_ref, left_ref, new_ref, mine_ref, theirs_ref,
                  tile_scr, half_scr, *, scale):
    block = where_ref[0]
    few = SUBS // 2
    for n, halves in enumerate(((near_ref, far_ref), (other_near_ref, other_far_ref))):
        for place in range(SHARDS):
            shard = jnp.bitwise_xor(where_ref[1 + n], place)
            ref, at = halves[place // 8], place % 8
            tile_scr[n, pl.ds(pl.multiple_of(shard * SUBS, SUBS), SUBS), :] = ref[at, 0]
            half_scr[n, shard] = ref[at, 1]
    rows, cols = places_in((LANES, LANES))
    corners, halves = [], []
    for n in range(2):
        tile = tile_scr[n]
        corners.append(jnp.where(cols > rows, tile.T, tile))
        halves.append(jnp.concatenate([half_scr[n, s, :few, :] for s in range(SHARDS)], 0))
    first = block == 0
    upper = jnp.concatenate([jnp.where(first, halves[0], halves[1]), jnp.where(first, halves[1], halves[0])], 0)
    stats = jnp.concatenate(
        [
            jnp.concatenate([jnp.where(first, corners[0], corners[1]), upper], 1),
            jnp.concatenate([upper.T, jnp.where(first, corners[1], corners[0])], 1),
        ],
        0,
    )
    new_ref[...] = 0.5 * fac_ref[...] + 0.5 * (stats * scale)
    rows, cols = places_in(new_ref.shape)
    damped = new_ref[...] + jnp.where(rows == cols, damping, 0.0)
    squares = jnp.sum(jnp.sum(damped * damped, axis=0, keepdims=True), axis=1, keepdims=True)
    over = 1.0 / jnp.sqrt(squares)
    scaled = damped * over
    first = split(scaled)
    twice = 2.0 * scaled - mul3(first, first)
    second = split(twice)
    fourth = split(2.0 * twice - mul3(second, second))
    head = jnp.where(rows == cols, 4.0, 0.0) - 2.0 * (scaled + twice) + mul3(first, second)
    inverse = split((2.0 * head - mul3(split(head), fourth)) * over)
    slab = mine_ref.shape[0]
    theirs_ref[...] = mul3(split(left_ref[pl.ds(pl.multiple_of((1 - block) * slab, SUBS), slab), :]), inverse)
    mine_ref[...] = mul3(split(left_ref[pl.ds(pl.multiple_of(block * slab, SUBS), slab), :]), inverse)


def call(kernel, where, args, outs, scratch=(), flops=0):
    size = sum(arg.size * arg.dtype.itemsize for arg in args) + sum(4 * math.prod(shape) for shape in outs)
    return pl.pallas_call(
        kernel,
        out_shape=[jax.ShapeDtypeStruct(shape, jnp.float32) for shape in outs],
        in_specs=[pl.BlockSpec(memory_space=pltpu.SMEM)]
        + [pl.BlockSpec(memory_space=pltpu.VMEM)] * len(args),
        out_specs=[pl.BlockSpec(memory_space=pltpu.VMEM)] * len(outs),
        scratch_shapes=[pltpu.VMEM(shape, jnp.float32) for shape in scratch],
        cost_estimate=pl.CostEstimate(flops=flops, bytes_accessed=size, transcendentals=0),
    )(where, *args)


def on_chip_pairs(activations, cotangents, input_factor, output_factor, gradient, weights, momentum):
    nblocks, slab, order = input_factor.shape
    rank = output_factor.shape[0]
    group = lax.axis_index("grp")
    spot = lax.axis_index("own")
    peers = lax.axis_size("own")
    samples = activations.shape[0] * lax.axis_size("grp") * peers
    scale = 1.0 / samples
    x_bit, y_bit, z_bits = spot % 2, (spot // 2) % 2, spot // 4
    straight = x_bit * 8 + y_bit * 4 + z_bits
    crossed = y_bit * 8 + x_bit * 4 + z_bits
    me = jnp.where(group == 0, straight, crossed)
    partner = jnp.where(group == 0, crossed, straight)
    where = jnp.stack([group, me, partner]).astype(jnp.int32)
    tiles = order // LANES
    packed = [(SHARDS, 2 + tiles * (tiles - 1) // 2 + (tiles + 1) // 2 - 1, SUBS, LANES)]
    heavy = 2 * order * order * (3 * order + 12 * rank)
    fence = lax.optimization_barrier

    def swap(value):
        return lax.ppermute(value, "grp", [(0, 1), (1, 0)])

    def send(value, flips):
        pairs = [(g * peers + o, g * peers + (o ^ flips[g])) for g in range(2) for o in range(peers)]
        return lax.ppermute(value, ("grp", "own"), pairs)

    def cross(value, flips):
        pairs = [(g * peers + o, (1 - g) * peers + (o ^ flips[g])) for g in range(2) for o in range(peers)]
        return lax.ppermute(value, ("grp", "own"), pairs)

    def stats(far):
        return call(lambda *refs: stats_kernel(*refs, far=far), where, (activations, cotangents), packed,
                    flops=2 * activations.shape[0] * order * order)[0]

    arrived = swap(stats(True))
    held = stats(False)
    going = held[8:] + arrived[8:]
    came = send(going, (1, 2))
    fac_rows, grad_rows, _ = fence((input_factor, gradient, going))
    fac_far = swap(lax.dynamic_index_in_dim(fac_rows, 1 - group, 0, False))
    grad_far = swap(lax.dynamic_index_in_dim(grad_rows, 1 - group, 0, False))
    came, fac_far, grad_far = fence((came, fac_far, grad_far))
    kept = held[:8] + arrived[:8]
    came = send(kept[4:] + came[4:], (2, 1)), kept[:4] + came[:4]
    kept = came[0] + came[1]
    ways = (3, 2, 1)
    pieces = {d: send(kept[d : d + 1], (4 * d, 4 * d)) for d in ways}
    kept = kept[:1] + pieces[3] + pieces[2] + pieces[1]
    pieces = {d: send(kept, (4 * d, 4 * d)) for d in ways}
    kept = jnp.concatenate([kept, pieces[1], pieces[2], pieces[3]], 0)
    near = jnp.concatenate([kept, send(kept, (2, 1))], 0)
    far = send(near, (1, 2))

    share = near[:, :2]
    beside = swap(share)
    across = cross(share, (1, 2))
    far, beside, across = fence((far, beside, across))
    mine, theirs, left = call(
        lambda *refs: input_kernel(*refs, scale=scale),
        where,
        (near, far, input_factor, fac_far, gradient, grad_far),
        [(slab, order), (slab, order), (order, rank)],
        [(packed[0][1], LANES, LANES), (order, order), (order, rank)],
        heavy,
    )
    new_output, update, update_far = call(
        lambda *refs: output_kernel(*refs, scale=scale),
        where,
        (near, far, beside, across, output_factor, left),
        [(rank, rank), (slab, rank), (slab, rank)],
        [(2, LANES, LANES), (2, SHARDS, SUBS, LANES)],
        24 * rank * rank * rank + 6 * order * rank * rank,
    )
    rows_far = swap(theirs)
    update_far = swap(update_far)
    own_block = lax.broadcasted_iota(jnp.int32, (nblocks, 1, 1), 0) == group
    new_input = jnp.where(own_block, mine[None], rows_far[None])
    update_far, _ = fence((update_far, new_input))
    new_momentum = mom_decay * momentum + jnp.where(own_block, update[None], update_far[None])
    new_weights = weights - step_size * new_momentum
    return (new_weights, new_momentum, new_input, new_output)


def solution(mesh):
    placed = (
        P(("grp", "own"), None),
        P(("grp", "own"), None),
        P(None, "grp", None),
        P(),
        P(None, "grp", None),
        P(None, "grp", None),
        P(None, "grp", None),
    )

    def on_device(*args):
        nblocks, slab, order = args[2].shape
        rank = args[3].shape[0]
        fits = nblocks == 2 and order % LANES == 0 and slab % SUBS == 0 and rank == 2 * LANES and order // LANES in (1, 3, 5, 7)
        paired = mesh.shape["grp"] == 2 and mesh.shape["own"] == SHARDS
        return (on_chip_pairs if fits and paired else any_mesh)(*args)

    return jax.shard_map(
        on_device,
        mesh=mesh,
        in_specs=placed,
        out_specs=(P(None, "grp", None), P(None, "grp", None), P(None, "grp", None), P()),
        check_vma=False,
    )
```

```python
import jax
import jax.numpy as jnp
from jax import lax
from jax.experimental import pallas as pl
from jax.experimental.pallas import tpu as pltpu
from jax.sharding import PartitionSpec as P

ITERS = 3


damping = 0.1
mom_decay = 0.9
step_size = 0.5

LANES = 128
SUBS = 8
SHARDS = 16


def newton_start(damped, ident):
    squares = jnp.sum(damped * damped, axis=(-2, -1), keepdims=True)
    bound = jnp.sqrt(squares)
    return 2.0 / bound * ident - damped / (bound * bound)


def step_rows(damped_rows, own_rows, full_iterate):
    product = jnp.matmul(damped_rows, full_iterate, precision=lax.Precision.HIGHEST)
    return 2.0 * own_rows - jnp.matmul(product, full_iterate, precision=lax.Precision.HIGHEST)


def any_mesh(activations, cotangents, input_factor, output_factor, gradient, weights, momentum):
    nblocks, slab, order = input_factor.shape
    rank = output_factor.shape[0]
    tokens = activations.shape[0]
    groups = lax.axis_size("grp")
    samples = tokens * groups * lax.axis_size("own")
    first_row = lax.axis_index("grp") * slab
    split_in = activations.reshape(tokens, nblocks, order)
    stat_in = jnp.einsum("tki,tkj->kij", split_in, split_in, preferred_element_type=jnp.float32)
    stat_out = jnp.einsum("ti,tj->ij", cotangents, cotangents, preferred_element_type=jnp.float32)
    total_in, total_out = lax.psum((stat_in, stat_out), ("grp", "own"))
    share_in = lax.dynamic_slice_in_dim(total_in, first_row, slab, 1)
    new_input = 0.5 * input_factor + 0.5 * (share_in / samples)
    new_output = 0.5 * output_factor + 0.5 * (total_out / samples)
    rows_in = lax.broadcasted_iota(jnp.int32, (slab, order), 0) + first_row
    cols_in = lax.broadcasted_iota(jnp.int32, (slab, order), 1)
    ident_rows = (rows_in == cols_in).astype(jnp.float32)
    ident_out = jnp.eye(rank, dtype=jnp.float32)
    damped_in = new_input + damping * ident_rows
    damped_out = new_output + damping * ident_out
    squares = lax.psum(jnp.sum(damped_in * damped_in, axis=(1, 2), keepdims=True), "grp")
    bound = jnp.sqrt(squares)
    iterate_in = 2.0 / bound * ident_rows - damped_in / (bound * bound)
    start_out = newton_start(damped_out, ident_out)
    out_rows = rank // groups
    first_out = lax.axis_index("grp") * out_rows
    damped_rows = lax.dynamic_slice_in_dim(damped_out, first_out, out_rows, 0)
    iterate_out = lax.dynamic_slice_in_dim(start_out, first_out, out_rows, 0)
    for iteration in range(ITERS - 1):
        full_in, full_out = (
            lax.all_gather(iterate_in, "grp", axis=1, tiled=True),
            lax.all_gather(iterate_out, "grp", axis=0, tiled=True),
        )
        iterate_in = step_rows(damped_in, iterate_in, full_in)
        iterate_out = step_rows(damped_rows, iterate_out, full_out)
    inverse_out = lax.all_gather(iterate_out, "grp", axis=0, tiled=True)
    precond = jnp.einsum(
        "kij,kjr->kir",
        iterate_in,
        lax.all_gather(gradient, "grp", axis=1, tiled=True),
        precision=lax.Precision.HIGHEST,
    )
    update = jnp.einsum("kir,rs->kis", precond, inverse_out, precision=lax.Precision.HIGHEST)
    new_momentum = mom_decay * momentum + update
    new_weights = weights - step_size * new_momentum
    return (new_weights, new_momentum, new_input, new_output)


def split(value):
    high = value.astype(jnp.bfloat16)
    low = (value - high.astype(jnp.float32)).astype(jnp.bfloat16)
    return high, low


def mul(a, b):
    return jnp.dot(a, b, preferred_element_type=jnp.float32)


def mul3(a, b):
    return mul(a[0], b[0]) + (mul(a[0], b[1]) + mul(a[1], b[0]))


def apply3(a, b):
    b = split(b)
    half = a[0].shape[0] // 2
    return jnp.concatenate([mul3([v[:half] for v in a], b), mul3([v[half:] for v in a], b)], 0)


def twice_less_square(value, halves):
    order = value.shape[0]
    ends = list(range(order, 0, -2 * LANES))[::-1]
    strips = []
    for end in ends:
        cols = slice(max(end - 2 * LANES, 0), end)
        square = mul3([v[:end] for v in halves], [v[:, cols] for v in halves])
        strips.append(split(2.0 * value[:end, cols] - square))
    parts = []
    for part in range(2):
        rows = []
        for n, end in enumerate(ends):
            top = ends[n - 1] if n else 0
            left = [strips[n][part][:top].T] if n else []
            right = [strips[m][part][top:end] for m in range(n, len(ends))]
            rows.append(jnp.concatenate(left + right, 1))
        parts.append(jnp.concatenate(rows, 0))
    return parts


def tile_pairs(tiles):
    return [(i, j) for i in range(tiles) for j in range(i, tiles)]


def places_in(shape):
    rows = lax.broadcasted_iota(jnp.int32, shape, 0)
    cols = lax.broadcasted_iota(jnp.int32, shape, 1)
    return rows, cols


def stats_kernel(where_ref, act_ref, cot_ref, packed_ref, *, far):
    block = 1 - where_ref[0] if far else where_ref[0]
    me = where_ref[2] if far else where_ref[1]
    order = act_ref.shape[1] // 2
    tiles = order // LANES
    places = [jnp.bitwise_xor(me, s) for s in range(SHARDS)]

    def put(index, tile):
        for s in range(SHARDS):
            packed_ref[places[s], index] = tile[s * SUBS : (s + 1) * SUBS]

    index = 2
    act = act_ref[:, pl.ds(pl.multiple_of(block * order, LANES), order)]
    turned = act.T
    diagonal = []
    for i in range(tiles):
        strip = mul(turned[i * LANES : (i + 1) * LANES], act[:, i * LANES :])
        diagonal.append(strip[:, :LANES])
        for j in range(1, tiles - i):
            put(index, strip[:, j * LANES : (j + 1) * LANES])
            index += 1
    cot = cot_ref[:, pl.ds(pl.multiple_of(block * LANES, LANES), LANES)]
    diagonal.append(mul(cot.T, cot))
    upper = mul(cot_ref[:, :LANES].T, cot_ref[:, LANES:])
    half = LANES // 2
    upper = jnp.where(block == 0, upper[:half], upper[half:])
    rows, cols = places_in((LANES, LANES))
    npairs = len(diagonal) // 2
    lines = []
    for pair in range(npairs):
        above, below = diagonal[2 * pair], diagonal[2 * pair + 1]
        put(index + pair if pair < npairs - 1 else 0, jnp.where(cols > rows, above, below))
        lines.append(jnp.sum(jnp.where(cols == rows, above, 0.0).reshape(SHARDS, SUBS, LANES), axis=1))
    few = SUBS // 2
    for s in range(SHARDS):
        packed_ref[places[s], 1, :few] = upper[s * few : (s + 1) * few]
        for pair in range(few):
            line = lines[pair][s : s + 1] if pair < npairs else jnp.zeros((1, LANES), jnp.float32)
            packed_ref[places[s], 1, few + pair : few + pair + 1] = line


def spread(me, halves, put):
    for place in range(SHARDS):
        half = halves[place * len(halves) // SHARDS]
        put(pl.multiple_of(jnp.bitwise_xor(me, place) * SUBS, SUBS), half[place % half.shape[0]])


def input_kernel(where_ref, near_ref, far_ref, fac_ref, fac_far_ref, grad_ref, grad_far_ref,
                 mine_ref, theirs_ref, left_ref, stat_ref, fac_scr, grad_scr, *, scale):
    block, me = where_ref[0], where_ref[1]
    slab, order = fac_far_ref.shape
    tiles = order // LANES
    own_rows = pl.ds(pl.multiple_of(block * slab, SUBS), slab)
    far_rows = pl.ds(pl.multiple_of((1 - block) * slab, SUBS), slab)
    def put(row, rows):
        stat_ref[:, pl.ds(row, SUBS), :] = rows

    spread(me, (near_ref, far_ref), put)
    fac_scr[own_rows, :] = 0.5 * fac_ref[block]
    fac_scr[far_rows, :] = 0.5 * fac_far_ref[...]
    grad_scr[own_rows, :] = grad_ref[block]
    grad_scr[far_rows, :] = grad_far_ref[...]
    at = lambda n: slice(n * LANES, (n + 1) * LANES)
    index = 2
    for i in range(tiles):
        for j in range(i + 1, tiles):
            part = 0.5 * (stat_ref[index] * scale)
            fac_scr[at(i), at(j)] += part
            fac_scr[at(j), at(i)] += part.T
            index += 1
    rows, cols = places_in((LANES, LANES))
    npairs = (tiles + 1) // 2
    for pair in range(npairs):
        part = 0.5 * (stat_ref[index + pair if pair < npairs - 1 else 0] * scale)
        turned = part.T
        line = stat_ref[1, pl.ds(SUBS // 2 + pair, SHARDS, stride=SUBS), :]
        line = 0.5 * (jnp.sum(line, axis=0, keepdims=True) * scale)
        above = jnp.where(cols > rows, part, jnp.where(cols < rows, turned, line))
        fac_scr[at(2 * pair), at(2 * pair)] += above
        if pair < npairs - 1:
            fac_scr[at(2 * pair + 1), at(2 * pair + 1)] += jnp.where(cols > rows, turned, part)
    mine_ref[...] = fac_scr[own_rows, :]
    theirs_ref[...] = fac_scr[far_rows, :]
    rows = lax.broadcasted_iota(jnp.int32, (order, order), 0)
    cols = lax.broadcasted_iota(jnp.int32, (order, order), 1)
    damped = fac_scr[...] + jnp.where(rows == cols, damping, 0.0)
    squares = jnp.sum(jnp.sum(damped * damped, axis=0, keepdims=True), axis=1, keepdims=True)
    over = 1.0 / jnp.sqrt(squares)
    scaled = damped * over
    first = split(scaled)
    twice = twice_less_square(scaled, first)
    grad = grad_scr[...]
    grad = 2.0 * grad - apply3(first, grad)
    grad = 2.0 * grad - apply3(twice, grad)
    once = grad - apply3(twice, grad)
    left_ref[...] = (grad + once - apply3(twice, once)) * over


def output_kernel(where_ref, near_ref, far_ref, other_near_ref, other_far_ref, fac_ref, left_ref, _, new_ref, mine_ref, theirs_ref,
                  tile_scr, half_scr, *, scale):
    block = where_ref[0]
    few = SUBS // 2
    for n, halves in enumerate(((near_ref, far_ref), (other_near_ref, other_far_ref))):
        for place in range(SHARDS):
            shard = jnp.bitwise_xor(where_ref[1 + n], place)
            ref, at = halves[place // 8], place % 8
            tile_scr[n, pl.ds(pl.multiple_of(shard * SUBS, SUBS), SUBS), :] = ref[at, 0]
            half_scr[n, shard] = ref[at, 1]
    rows, cols = places_in((LANES, LANES))
    corners, halves = [], []
    for n in range(2):
        tile = tile_scr[n]
        corners.append(jnp.where(cols > rows, tile.T, tile))
        halves.append(jnp.concatenate([half_scr[n, s, :few, :] for s in range(SHARDS)], 0))
    first = block == 0
    upper = jnp.concatenate([jnp.where(first, halves[0], halves[1]), jnp.where(first, halves[1], halves[0])], 0)
    stats = jnp.concatenate(
        [
            jnp.concatenate([jnp.where(first, corners[0], corners[1]), upper], 1),
            jnp.concatenate([upper.T, jnp.where(first, corners[1], corners[0])], 1),
        ],
        0,
    )
    new_ref[...] = 0.5 * fac_ref[...] + 0.5 * (stats * scale)
    rows, cols = places_in(new_ref.shape)
    damped = new_ref[...] + jnp.where(rows == cols, damping, 0.0)
    squares = jnp.sum(jnp.sum(damped * damped, axis=0, keepdims=True), axis=1, keepdims=True)
    over = 1.0 / jnp.sqrt(squares)
    scaled = damped * over
    first = split(scaled)
    twice = 2.0 * scaled - mul3(first, first)
    second = split(twice)
    fourth = split(2.0 * twice - mul3(second, second))
    head = jnp.where(rows == cols, 4.0, 0.0) - 2.0 * (scaled + twice) + mul3(first, second)
    inverse = split((2.0 * head - mul3(split(head), fourth)) * over)
    slab = mine_ref.shape[0]
    theirs_ref[...] = mul3(split(left_ref[pl.ds(pl.multiple_of((1 - block) * slab, SUBS), slab), :]), inverse)
    mine_ref[...] = mul3(split(left_ref[pl.ds(pl.multiple_of(block * slab, SUBS), slab), :]), inverse)


def call(kernel, where, args, outs, scratch=(), flops=0):
    outs = [jax.ShapeDtypeStruct(shape, jnp.float32) for shape in outs]
    size = sum(array.size * array.dtype.itemsize for array in (*args, *outs))
    return pl.pallas_call(
        kernel,
        out_shape=outs,
        in_specs=[pl.BlockSpec(memory_space=pltpu.SMEM)] + [pl.BlockSpec(memory_space=pltpu.VMEM)] * len(args),
        out_specs=[pl.BlockSpec(memory_space=pltpu.VMEM)] * len(outs),
        scratch_shapes=[pltpu.VMEM(shape, jnp.float32) for shape in scratch],
        compiler_params=pltpu.CompilerParams(vmem_limit_bytes=24 << 20),
        cost_estimate=pl.CostEstimate(flops=flops, bytes_accessed=size, transcendentals=0),
    )(where, *args)


def on_chip_pairs(activations, cotangents, input_factor, output_factor, gradient, weights, momentum):
    nblocks, slab, order = input_factor.shape
    rank = output_factor.shape[0]
    group = lax.axis_index("grp")
    spot = lax.axis_index("own")
    peers = lax.axis_size("own")
    samples = activations.shape[0] * lax.axis_size("grp") * peers
    scale = 1.0 / samples
    x_bit, y_bit, z_bits = spot % 2, (spot // 2) % 2, spot // 4
    straight = x_bit * 8 + y_bit * 4 + z_bits
    crossed = y_bit * 8 + x_bit * 4 + z_bits
    me = jnp.where(group == 0, straight, crossed)
    partner = jnp.where(group == 0, crossed, straight)
    where = jnp.stack([group, me, partner]).astype(jnp.int32)
    tiles = order // LANES
    packed = [(SHARDS, 2 + tiles * (tiles - 1) // 2 + (tiles + 1) // 2 - 1, SUBS, LANES)]
    heavy = 2 * order * order * (3 * order + 12 * rank)
    fence = lax.optimization_barrier

    def swap(value):
        return lax.ppermute(value, "grp", [(0, 1), (1, 0)])

    def send(value, flips):
        pairs = [(g * peers + o, g * peers + (o ^ flips[g])) for g in range(2) for o in range(peers)]
        return lax.ppermute(value, ("grp", "own"), pairs)

    def cross(value, flips):
        pairs = [(g * peers + o, (1 - g) * peers + (o ^ flips[g])) for g in range(2) for o in range(peers)]
        return lax.ppermute(value, ("grp", "own"), pairs)

    samples_in = (activations, cotangents)
    work = 2 * activations.shape[0] * order * order
    (theirs,) = call(lambda *refs: stats_kernel(*refs, far=True), where, samples_in, packed, (), work)
    arrived = swap(theirs[8:]), swap(theirs[:8])
    (held,) = call(lambda *refs: stats_kernel(*refs, far=False), where, samples_in, packed, (), work)
    going = held[8:] + arrived[0]
    kept = held[:8] + arrived[1]
    came = send(going, (1, 2))
    fac_rows, grad_rows, kept = fence((input_factor, gradient, kept))
    fac_far = swap(lax.dynamic_index_in_dim(fac_rows, 1 - group, 0, False))
    grad_far = swap(lax.dynamic_index_in_dim(grad_rows, 1 - group, 0, False))
    came, fac_far, grad_far = fence((came, fac_far, grad_far))
    came = send(kept[4:] + came[4:], (2, 1)), kept[:4] + came[:4]
    kept = came[0] + came[1]
    ways = (3, 2, 1)
    pieces = {d: send(kept[d : d + 1], (4 * d, 4 * d)) for d in ways}
    kept = kept[:1] + pieces[3] + pieces[2] + pieces[1]
    pieces = {d: send(kept, (4 * d, 4 * d)) for d in ways}
    pace = swap(pieces[3][:, :1])
    kept = jnp.concatenate([kept, pieces[1], pieces[2], pieces[3]], 0)
    kept, pace = fence((kept, pace))
    near = jnp.concatenate([kept, send(kept, (2, 1))], 0)
    far = send(near, (1, 2))

    share = near[:, :2]
    beside = swap(share)
    across = cross(share, (1, 2))
    far, beside, across = fence((far, beside, across))
    mine, theirs, left = call(
        lambda *refs: input_kernel(*refs, scale=scale),
        where,
        (near, far, input_factor, fac_far, gradient, grad_far),
        [(slab, order), (slab, order), (order, rank)],
        [(packed[0][1], LANES, LANES), (order, order), (order, rank)],
        heavy,
    )
    new_output, update, update_far = call(
        lambda *refs: output_kernel(*refs, scale=scale),
        where,
        (near, far, beside, across, output_factor, left, pace),
        [(rank, rank), (slab, rank), (slab, rank)],
        [(2, LANES, LANES), (2, SHARDS, SUBS, LANES)],
        24 * rank * rank * rank + 6 * order * rank * rank,
    )
    rows_far = swap(theirs)
    update_far = swap(update_far)
    own_block = lax.broadcasted_iota(jnp.int32, (nblocks, 1, 1), 0) == group
    new_input = jnp.where(own_block, mine[None], rows_far[None])
    update_far, _ = fence((update_far, new_input))
    new_momentum = mom_decay * momentum + jnp.where(own_block, update[None], update_far[None])
    new_weights = weights - step_size * new_momentum
    return (new_weights, new_momentum, new_input, new_output)


def solution(mesh):
    placed = (
        P(("grp", "own"), None),
        P(("grp", "own"), None),
        P(None, "grp", None),
        P(),
        P(None, "grp", None),
        P(None, "grp", None),
        P(None, "grp", None),
    )

    def on_device(*args):
        nblocks, slab, order = args[2].shape
        rank = args[3].shape[0]
        fits = nblocks == 2 and order % LANES == 0 and slab % SUBS == 0 and rank == 2 * LANES and order // LANES in (1, 3, 5, 7)
        paired = mesh.shape["grp"] == 2 and mesh.shape["own"] == SHARDS
        return (on_chip_pairs if fits and paired else any_mesh)(*args)

    return jax.shard_map(
        on_device,
        mesh=mesh,
        in_specs=placed,
        out_specs=(P(None, "grp", None), P(None, "grp", None), P(None, "grp", None), P()),
        check_vma=False,
    )
```

```python
import jax
import jax.numpy as jnp
from jax import lax
from jax.experimental import pallas as pl
from jax.experimental.pallas import tpu as pltpu
from jax.sharding import PartitionSpec as P

ITERS = 3


damping = 0.1
mom_decay = 0.9
step_size = 0.5

LANES = 128
SUBS = 8
SHARDS = 16


def newton_start(damped, ident):
    squares = jnp.sum(damped * damped, axis=(-2, -1), keepdims=True)
    bound = jnp.sqrt(squares)
    return 2.0 / bound * ident - damped / (bound * bound)


def step_rows(damped_rows, own_rows, full_iterate):
    product = jnp.matmul(damped_rows, full_iterate, precision=lax.Precision.HIGHEST)
    return 2.0 * own_rows - jnp.matmul(product, full_iterate, precision=lax.Precision.HIGHEST)


def any_mesh(activations, cotangents, input_factor, output_factor, gradient, weights, momentum):
    nblocks, slab, order = input_factor.shape
    rank = output_factor.shape[0]
    tokens = activations.shape[0]
    groups = lax.axis_size("grp")
    samples = tokens * groups * lax.axis_size("own")
    first_row = lax.axis_index("grp") * slab
    split_in = activations.reshape(tokens, nblocks, order)
    stat_in = jnp.einsum("tki,tkj->kij", split_in, split_in, preferred_element_type=jnp.float32)
    stat_out = jnp.einsum("ti,tj->ij", cotangents, cotangents, preferred_element_type=jnp.float32)
    total_in, total_out = lax.psum((stat_in, stat_out), ("grp", "own"))
    share_in = lax.dynamic_slice_in_dim(total_in, first_row, slab, 1)
    new_input = 0.5 * input_factor + 0.5 * (share_in / samples)
    new_output = 0.5 * output_factor + 0.5 * (total_out / samples)
    rows_in = lax.broadcasted_iota(jnp.int32, (slab, order), 0) + first_row
    cols_in = lax.broadcasted_iota(jnp.int32, (slab, order), 1)
    ident_rows = (rows_in == cols_in).astype(jnp.float32)
    ident_out = jnp.eye(rank, dtype=jnp.float32)
    damped_in = new_input + damping * ident_rows
    damped_out = new_output + damping * ident_out
    squares = lax.psum(jnp.sum(damped_in * damped_in, axis=(1, 2), keepdims=True), "grp")
    bound = jnp.sqrt(squares)
    iterate_in = 2.0 / bound * ident_rows - damped_in / (bound * bound)
    start_out = newton_start(damped_out, ident_out)
    out_rows = rank // groups
    first_out = lax.axis_index("grp") * out_rows
    damped_rows = lax.dynamic_slice_in_dim(damped_out, first_out, out_rows, 0)
    iterate_out = lax.dynamic_slice_in_dim(start_out, first_out, out_rows, 0)
    for iteration in range(ITERS - 1):
        full_in, full_out = (
            lax.all_gather(iterate_in, "grp", axis=1, tiled=True),
            lax.all_gather(iterate_out, "grp", axis=0, tiled=True),
        )
        iterate_in = step_rows(damped_in, iterate_in, full_in)
        iterate_out = step_rows(damped_rows, iterate_out, full_out)
    inverse_out = lax.all_gather(iterate_out, "grp", axis=0, tiled=True)
    precond = jnp.einsum(
        "kij,kjr->kir",
        iterate_in,
        lax.all_gather(gradient, "grp", axis=1, tiled=True),
        precision=lax.Precision.HIGHEST,
    )
    update = jnp.einsum("kir,rs->kis", precond, inverse_out, precision=lax.Precision.HIGHEST)
    new_momentum = mom_decay * momentum + update
    new_weights = weights - step_size * new_momentum
    return (new_weights, new_momentum, new_input, new_output)


def split(value):
    high = value.astype(jnp.bfloat16)
    low = (value - high.astype(jnp.float32)).astype(jnp.bfloat16)
    return high, low


def mul(a, b):
    return jnp.dot(a, b, preferred_element_type=jnp.float32)


def mul3(a, b):
    return mul(a[0], b[0]) + (mul(a[0], b[1]) + mul(a[1], b[0]))


def long3(a, b):
    return mul(jnp.concatenate([a[0], a[1], a[0]], 1), jnp.concatenate([b[0], b[0], b[1]], 0))


def apply3(a, b):
    b = split(b)
    half = a[0].shape[0] // 2
    return jnp.concatenate([long3([v[:half] for v in a], b), long3([v[half:] for v in a], b)], 0)


def twice_less_square(value, halves):
    order = value.shape[0]
    ends = list(range(order, 0, -2 * LANES))[::-1]
    strips = []
    for end in ends:
        cols = slice(max(end - 2 * LANES, 0), end)
        square = long3([v[:end] for v in halves], [v[:, cols] for v in halves])
        strips.append(split(2.0 * value[:end, cols] - square))
    parts = []
    for part in range(2):
        rows = []
        for n, end in enumerate(ends):
            top = ends[n - 1] if n else 0
            left = [strips[n][part][:top].T] if n else []
            right = [strips[m][part][top:end] for m in range(n, len(ends))]
            rows.append(jnp.concatenate(left + right, 1))
        parts.append(jnp.concatenate(rows, 0))
    return parts


def tile_pairs(tiles):
    return [(i, j) for i in range(tiles) for j in range(i, tiles)]


def places_in(shape):
    rows = lax.broadcasted_iota(jnp.int32, shape, 0)
    cols = lax.broadcasted_iota(jnp.int32, shape, 1)
    return rows, cols


def stats_kernel(where_ref, act_ref, out_ref, packed_ref, *, far):
    block = 1 - where_ref[0] if far else where_ref[0]
    me = where_ref[2] if far else where_ref[1]
    order = act_ref.shape[1] // 2
    tiles = order // LANES
    places = [jnp.bitwise_xor(me, s) for s in range(SHARDS)]

    def put(index, tile):
        for s in range(SHARDS):
            packed_ref[places[s], index] = tile[s * SUBS : (s + 1) * SUBS]

    index = 2
    act = act_ref[:, pl.ds(pl.multiple_of(block * order, LANES), order)]
    turned = act.T
    diagonal = []
    for i in range(tiles):
        strip = mul(turned[i * LANES : (i + 1) * LANES], act[:, i * LANES :])
        diagonal.append(strip[:, :LANES])
        for j in range(1, tiles - i):
            put(index, strip[:, j * LANES : (j + 1) * LANES])
            index += 1
    here = pl.ds(pl.multiple_of(block * LANES, LANES), LANES)
    diagonal.append(out_ref[here, here])
    half = LANES // 2
    upper = out_ref[pl.ds(pl.multiple_of(block * half, SUBS), half), LANES:]
    rows, cols = places_in((LANES, LANES))
    npairs = len(diagonal) // 2
    lines = []
    for pair in range(npairs):
        above, below = diagonal[2 * pair], diagonal[2 * pair + 1]
        put(index + pair if pair < npairs - 1 else 0, jnp.where(cols > rows, above, below))
        lines.append(jnp.sum(jnp.where(cols == rows, above, 0.0).reshape(SHARDS, SUBS, LANES), axis=1))
    few = SUBS // 2
    for s in range(SHARDS):
        packed_ref[places[s], 1, :few] = upper[s * few : (s + 1) * few]
        for pair in range(few):
            line = lines[pair][s : s + 1] if pair < npairs else jnp.zeros((1, LANES), jnp.float32)
            packed_ref[places[s], 1, few + pair : few + pair + 1] = line


def spread(me, halves, put):
    for place in range(SHARDS):
        half = halves[place * len(halves) // SHARDS]
        put(pl.multiple_of(jnp.bitwise_xor(me, place) * SUBS, SUBS), half[place % half.shape[0]])


def input_kernel(where_ref, near_ref, far_ref, fac_ref, fac_top_ref, fac_low_ref, grad_ref, grad_far_ref,
                 mine_ref, theirs_ref, left_ref, stat_ref, fac_scr, grad_scr, *, scale):
    block, me = where_ref[0], where_ref[1]
    slab, order = fac_ref.shape[1:]
    tiles = order // LANES
    own_rows = pl.ds(pl.multiple_of(block * slab, SUBS), slab)
    far_rows = pl.ds(pl.multiple_of((1 - block) * slab, SUBS), slab)
    def put(row, rows):
        stat_ref[:, pl.ds(row, SUBS), :] = rows

    spread(me, (near_ref, far_ref), put)
    fac_scr[own_rows, :] = 0.5 * fac_ref[block]
    for part, ref in enumerate((fac_top_ref, fac_low_ref)):
        first = (1 - block) * slab + part * (slab // 2)
        fac_scr[pl.ds(pl.multiple_of(first, SUBS), slab // 2), :] = 0.5 * ref[...]
    grad_scr[own_rows, :] = grad_ref[block]
    grad_scr[far_rows, :] = grad_far_ref[...]
    at = lambda n: slice(n * LANES, (n + 1) * LANES)
    index = 2
    for i in range(tiles):
        for j in range(i + 1, tiles):
            part = 0.5 * (stat_ref[index] * scale)
            fac_scr[at(i), at(j)] += part
            fac_scr[at(j), at(i)] += part.T
            index += 1
    rows, cols = places_in((LANES, LANES))
    npairs = (tiles + 1) // 2
    for pair in range(npairs):
        part = 0.5 * (stat_ref[index + pair if pair < npairs - 1 else 0] * scale)
        turned = part.T
        line = stat_ref[1, pl.ds(SUBS // 2 + pair, SHARDS, stride=SUBS), :]
        line = 0.5 * (jnp.sum(line, axis=0, keepdims=True) * scale)
        above = jnp.where(cols > rows, part, jnp.where(cols < rows, turned, line))
        fac_scr[at(2 * pair), at(2 * pair)] += above
        if pair < npairs - 1:
            fac_scr[at(2 * pair + 1), at(2 * pair + 1)] += jnp.where(cols > rows, turned, part)
    mine_ref[...] = fac_scr[own_rows, :]
    theirs_ref[...] = fac_scr[far_rows, :]
    rows = lax.broadcasted_iota(jnp.int32, (order, order), 0)
    cols = lax.broadcasted_iota(jnp.int32, (order, order), 1)
    damped = fac_scr[...] + jnp.where(rows == cols, damping, 0.0)
    squares = jnp.sum(jnp.sum(damped * damped, axis=0, keepdims=True), axis=1, keepdims=True)
    over = 1.0 / jnp.sqrt(squares)
    scaled = damped * over
    first = split(scaled)
    twice = twice_less_square(scaled, first)
    grad = grad_scr[...]
    grad = 2.0 * grad - apply3(first, grad)
    grad = 2.0 * grad - apply3(twice, grad)
    once = grad - apply3(twice, grad)
    left_ref[...] = (grad + once - apply3(twice, once)) * over


def output_kernel(where_ref, near_ref, far_ref, other_near_ref, other_far_ref, fac_ref, left_ref, _, new_ref, mine_ref, theirs_ref,
                  tile_scr, half_scr, *, scale):
    block = where_ref[0]
    few = SUBS // 2
    for n, halves in enumerate(((near_ref, far_ref), (other_near_ref, other_far_ref))):
        for place in range(SHARDS):
            shard = jnp.bitwise_xor(where_ref[1 + n], place)
            ref, at = halves[place // 8], place % 8
            tile_scr[n, pl.ds(pl.multiple_of(shard * SUBS, SUBS), SUBS), :] = ref[at, 0]
            half_scr[n, shard] = ref[at, 1]
    rows, cols = places_in((LANES, LANES))
    corners, halves = [], []
    for n in range(2):
        tile = tile_scr[n]
        corners.append(jnp.where(cols > rows, tile.T, tile))
        halves.append(jnp.concatenate([half_scr[n, s, :few, :] for s in range(SHARDS)], 0))
    first = block == 0
    upper = jnp.concatenate([jnp.where(first, halves[0], halves[1]), jnp.where(first, halves[1], halves[0])], 0)
    stats = jnp.concatenate(
        [
            jnp.concatenate([jnp.where(first, corners[0], corners[1]), upper], 1),
            jnp.concatenate([upper.T, jnp.where(first, corners[1], corners[0])], 1),
        ],
        0,
    )
    new_ref[...] = 0.5 * fac_ref[...] + 0.5 * (stats * scale)
    rows, cols = places_in(new_ref.shape)
    damped = new_ref[...] + jnp.where(rows == cols, damping, 0.0)
    squares = jnp.sum(jnp.sum(damped * damped, axis=0, keepdims=True), axis=1, keepdims=True)
    over = 1.0 / jnp.sqrt(squares)
    scaled = damped * over
    first = split(scaled)
    twice = 2.0 * scaled - mul3(first, first)
    second = split(twice)
    fourth = split(2.0 * twice - mul3(second, second))
    head = jnp.where(rows == cols, 4.0, 0.0) - 2.0 * (scaled + twice) + mul3(first, second)
    inverse = split((2.0 * head - mul3(split(head), fourth)) * over)
    slab = mine_ref.shape[0]
    theirs_ref[...] = mul3(split(left_ref[pl.ds(pl.multiple_of((1 - block) * slab, SUBS), slab), :]), inverse)
    mine_ref[...] = mul3(split(left_ref[pl.ds(pl.multiple_of(block * slab, SUBS), slab), :]), inverse)


def call(kernel, where, args, outs, scratch=(), flops=0):
    outs = [jax.ShapeDtypeStruct(shape, jnp.float32) for shape in outs]
    size = sum(array.size * array.dtype.itemsize for array in (*args, *outs))
    return pl.pallas_call(
        kernel,
        out_shape=outs,
        in_specs=[pl.BlockSpec(memory_space=pltpu.SMEM)] + [pl.BlockSpec(memory_space=pltpu.VMEM)] * len(args),
        out_specs=[pl.BlockSpec(memory_space=pltpu.VMEM)] * len(outs),
        scratch_shapes=[pltpu.VMEM(shape, jnp.float32) for shape in scratch],
        compiler_params=pltpu.CompilerParams(vmem_limit_bytes=24 << 20),
        cost_estimate=pl.CostEstimate(flops=flops, bytes_accessed=size, transcendentals=0),
    )(where, *args)


def on_chip_pairs(activations, cotangents, input_factor, output_factor, gradient, weights, momentum):
    nblocks, slab, order = input_factor.shape
    rank = output_factor.shape[0]
    group = lax.axis_index("grp")
    spot = lax.axis_index("own")
    peers = lax.axis_size("own")
    samples = activations.shape[0] * lax.axis_size("grp") * peers
    scale = 1.0 / samples
    x_bit, y_bit, z_bits = spot % 2, (spot // 2) % 2, spot // 4
    straight = x_bit * 8 + y_bit * 4 + z_bits
    crossed = y_bit * 8 + x_bit * 4 + z_bits
    me = jnp.where(group == 0, straight, crossed)
    partner = jnp.where(group == 0, crossed, straight)
    where = jnp.stack([group, me, partner]).astype(jnp.int32)
    tiles = order // LANES
    packed = [(SHARDS, 2 + tiles * (tiles - 1) // 2 + (tiles + 1) // 2 - 1, SUBS, LANES)]
    heavy = 2 * order * order * (3 * order + 12 * rank)
    fence = lax.optimization_barrier

    def swap(value):
        return lax.ppermute(value, "grp", [(0, 1), (1, 0)])

    def send(value, flips):
        pairs = [(g * peers + o, g * peers + (o ^ flips[g])) for g in range(2) for o in range(peers)]
        return lax.ppermute(value, ("grp", "own"), pairs)

    def cross(value, flips):
        pairs = [(g * peers + o, (1 - g) * peers + (o ^ flips[g])) for g in range(2) for o in range(peers)]
        return lax.ppermute(value, ("grp", "own"), pairs)

    stat_out = jnp.einsum("ti,tj->ij", cotangents, cotangents, preferred_element_type=jnp.float32)
    samples_in = (activations, stat_out)
    work = 2 * activations.shape[0] * order * order
    (theirs,) = call(lambda *refs: stats_kernel(*refs, far=True), where, samples_in, packed, (), work)
    arrived = swap(theirs[8:]), swap(theirs[:8])
    (held,) = call(lambda *refs: stats_kernel(*refs, far=False), where, samples_in, packed, (), work)
    going = held[8:] + arrived[0]
    kept = held[:8] + arrived[1]
    came = send(going, (1, 2))
    fac_rows = lax.dynamic_index_in_dim(input_factor, 1 - group, 0, False)
    grad_rows = lax.dynamic_index_in_dim(gradient, 1 - group, 0, False)
    fac_far = swap(fac_rows[: slab // 2]), swap(fac_rows[slab // 2 :])
    grad_far = swap(grad_rows)
    came, fac_far, grad_far = fence((came, fac_far, grad_far))
    came = send(kept[4:] + came[4:], (2, 1)), kept[:4] + came[:4]
    kept = came[0] + came[1]
    ways = (3, 2, 1)
    pieces = {d: send(kept[d : d + 1], (4 * d, 4 * d)) for d in ways}
    kept = kept[:1] + pieces[3] + pieces[2] + pieces[1]
    pieces = {d: send(kept, (4 * d, 4 * d)) for d in ways}
    pace = swap(pieces[3][:, :1])
    kept = jnp.concatenate([kept, pieces[1], pieces[2], pieces[3]], 0)
    kept, pace = fence((kept, pace))
    near = jnp.concatenate([kept, send(kept, (2, 1))], 0)
    far = send(near, (1, 2))
    share = near[:, :2]
    beside = swap(share)
    across = cross(share, (1, 2))
    far, beside, across = fence((far, beside, across))
    mine, theirs, left = call(
        lambda *refs: input_kernel(*refs, scale=scale),
        where,
        (near, far, input_factor, *fac_far, gradient, grad_far),
        [(slab, order), (slab, order), (order, rank)],
        [(packed[0][1], LANES, LANES), (order, order), (order, rank)],
        heavy,
    )
    new_output, update, update_far = call(
        lambda *refs: output_kernel(*refs, scale=scale),
        where,
        (near, far, beside, across, output_factor, left, pace),
        [(rank, rank), (slab, rank), (slab, rank)],
        [(2, LANES, LANES), (2, SHARDS, SUBS, LANES)],
        24 * rank * rank * rank + 6 * order * rank * rank,
    )
    rows_far = swap(theirs)
    update_far = swap(update_far)
    own_block = lax.broadcasted_iota(jnp.int32, (nblocks, 1, 1), 0) == group
    new_input = jnp.where(own_block, mine[None], rows_far[None])
    update_far, _ = fence((update_far, new_input))
    new_momentum = mom_decay * momentum + jnp.where(own_block, update[None], update_far[None])
    new_weights = weights - step_size * new_momentum
    return (new_weights, new_momentum, new_input, new_output)


def solution(mesh):
    placed = (
        P(("grp", "own"), None),
        P(("grp", "own"), None),
        P(None, "grp", None),
        P(),
        P(None, "grp", None),
        P(None, "grp", None),
        P(None, "grp", None),
    )

    def on_device(*args):
        nblocks, slab, order = args[2].shape
        rank = args[3].shape[0]
        fits = nblocks == 2 and order % LANES == 0 and slab % (2 * SUBS) == 0 and rank == 2 * LANES and order // LANES in (1, 3, 5, 7)
        paired = mesh.shape["grp"] == 2 and mesh.shape["own"] == SHARDS
        return (on_chip_pairs if fits and paired else any_mesh)(*args)

    return jax.shard_map(
        on_device,
        mesh=mesh,
        in_specs=placed,
        out_specs=(P(None, "grp", None), P(None, "grp", None), P(None, "grp", None), P()),
        check_vma=False,
    )
```

```python
import jax
import jax.numpy as jnp
from jax import lax
from jax.experimental import pallas as pl
from jax.experimental.pallas import tpu as pltpu
from jax.sharding import PartitionSpec as P

ITERS = 3


damping = 0.1
mom_decay = 0.9
step_size = 0.5

LANES = 128
SUBS = 8
SHARDS = 16


def newton_start(damped, ident):
    squares = jnp.sum(damped * damped, axis=(-2, -1), keepdims=True)
    bound = jnp.sqrt(squares)
    return 2.0 / bound * ident - damped / (bound * bound)


def step_rows(damped_rows, own_rows, full_iterate):
    product = jnp.matmul(damped_rows, full_iterate, precision=lax.Precision.HIGHEST)
    return 2.0 * own_rows - jnp.matmul(product, full_iterate, precision=lax.Precision.HIGHEST)


def any_mesh(activations, cotangents, input_factor, output_factor, gradient, weights, momentum):
    nblocks, slab, order = input_factor.shape
    rank = output_factor.shape[0]
    tokens = activations.shape[0]
    groups = lax.axis_size("grp")
    samples = tokens * groups * lax.axis_size("own")
    first_row = lax.axis_index("grp") * slab
    split_in = activations.reshape(tokens, nblocks, order)
    stat_in = jnp.einsum("tki,tkj->kij", split_in, split_in, preferred_element_type=jnp.float32)
    stat_out = jnp.einsum("ti,tj->ij", cotangents, cotangents, preferred_element_type=jnp.float32)
    total_in, total_out = lax.psum((stat_in, stat_out), ("grp", "own"))
    share_in = lax.dynamic_slice_in_dim(total_in, first_row, slab, 1)
    new_input = 0.5 * input_factor + 0.5 * (share_in / samples)
    new_output = 0.5 * output_factor + 0.5 * (total_out / samples)
    rows_in = lax.broadcasted_iota(jnp.int32, (slab, order), 0) + first_row
    cols_in = lax.broadcasted_iota(jnp.int32, (slab, order), 1)
    ident_rows = (rows_in == cols_in).astype(jnp.float32)
    ident_out = jnp.eye(rank, dtype=jnp.float32)
    damped_in = new_input + damping * ident_rows
    damped_out = new_output + damping * ident_out
    squares = lax.psum(jnp.sum(damped_in * damped_in, axis=(1, 2), keepdims=True), "grp")
    bound = jnp.sqrt(squares)
    iterate_in = 2.0 / bound * ident_rows - damped_in / (bound * bound)
    start_out = newton_start(damped_out, ident_out)
    out_rows = rank // groups
    first_out = lax.axis_index("grp") * out_rows
    damped_rows = lax.dynamic_slice_in_dim(damped_out, first_out, out_rows, 0)
    iterate_out = lax.dynamic_slice_in_dim(start_out, first_out, out_rows, 0)
    for iteration in range(ITERS - 1):
        full_in, full_out = (
            lax.all_gather(iterate_in, "grp", axis=1, tiled=True),
            lax.all_gather(iterate_out, "grp", axis=0, tiled=True),
        )
        iterate_in = step_rows(damped_in, iterate_in, full_in)
        iterate_out = step_rows(damped_rows, iterate_out, full_out)
    inverse_out = lax.all_gather(iterate_out, "grp", axis=0, tiled=True)
    precond = jnp.einsum(
        "kij,kjr->kir",
        iterate_in,
        lax.all_gather(gradient, "grp", axis=1, tiled=True),
        precision=lax.Precision.HIGHEST,
    )
    update = jnp.einsum("kir,rs->kis", precond, inverse_out, precision=lax.Precision.HIGHEST)
    new_momentum = mom_decay * momentum + update
    new_weights = weights - step_size * new_momentum
    return (new_weights, new_momentum, new_input, new_output)


def split(value):
    high = value.astype(jnp.bfloat16)
    low = (value - high.astype(jnp.float32)).astype(jnp.bfloat16)
    return high, low


def mul(a, b):
    return jnp.dot(a, b, preferred_element_type=jnp.float32)


def mul3(a, b):
    return mul(a[0], b[0]) + (mul(a[0], b[1]) + mul(a[1], b[0]))


def long3(a, b):
    return mul(jnp.concatenate([a[0], a[1], a[0]], 1), jnp.concatenate([b[0], b[0], b[1]], 0))


def apply3(a, b):
    b = split(b)
    half = a[0].shape[0] // 2
    return jnp.concatenate([long3([v[:half] for v in a], b), long3([v[half:] for v in a], b)], 0)


def twice_less_square(value, halves):
    order = value.shape[0]
    ends = list(range(order, 0, -2 * LANES))[::-1]
    strips = []
    for end in ends:
        cols = slice(max(end - 2 * LANES, 0), end)
        square = long3([v[:end] for v in halves], [v[:, cols] for v in halves])
        strips.append(split(2.0 * value[:end, cols] - square))
    parts = []
    for part in range(2):
        rows = []
        for n, end in enumerate(ends):
            top = ends[n - 1] if n else 0
            left = [strips[n][part][:top].T] if n else []
            right = [strips[m][part][top:end] for m in range(n, len(ends))]
            rows.append(jnp.concatenate(left + right, 1))
        parts.append(jnp.concatenate(rows, 0))
    return parts


def tile_pairs(tiles):
    return [(i, j) for i in range(tiles) for j in range(i, tiles)]


def places_in(shape):
    rows = lax.broadcasted_iota(jnp.int32, shape, 0)
    cols = lax.broadcasted_iota(jnp.int32, shape, 1)
    return rows, cols


def stats_kernel(where_ref, act_ref, out_ref, packed_ref, *, far):
    block = 1 - where_ref[0] if far else where_ref[0]
    me = where_ref[2] if far else where_ref[1]
    order = act_ref.shape[1] // 2
    tiles = order // LANES
    places = [jnp.bitwise_xor(me, s) for s in range(SHARDS)]

    def put(index, tile):
        for s in range(SHARDS):
            packed_ref[places[s], index] = tile[s * SUBS : (s + 1) * SUBS]

    index = 2
    act = act_ref[:, pl.ds(pl.multiple_of(block * order, LANES), order)]
    turned = act.T
    diagonal = []
    for i in range(tiles):
        strip = mul(turned[i * LANES : (i + 1) * LANES], act[:, i * LANES :])
        diagonal.append(strip[:, :LANES])
        for j in range(1, tiles - i):
            put(index, strip[:, j * LANES : (j + 1) * LANES])
            index += 1
    here = pl.ds(pl.multiple_of(block * LANES, LANES), LANES)
    diagonal.append(out_ref[here, here])
    half = LANES // 2
    upper = out_ref[pl.ds(pl.multiple_of(block * half, SUBS), half), LANES:]
    rows, cols = places_in((LANES, LANES))
    npairs = len(diagonal) // 2
    lines = []
    for pair in range(npairs):
        above, below = diagonal[2 * pair], diagonal[2 * pair + 1]
        put(index + pair if pair < npairs - 1 else 0, jnp.where(cols > rows, above, below))
        lines.append(jnp.sum(jnp.where(cols == rows, above, 0.0).reshape(SHARDS, SUBS, LANES), axis=1))
    few = SUBS // 2
    for s in range(SHARDS):
        packed_ref[places[s], 1, :few] = upper[s * few : (s + 1) * few]
        for pair in range(few):
            line = lines[pair][s : s + 1] if pair < npairs else jnp.zeros((1, LANES), jnp.float32)
            packed_ref[places[s], 1, few + pair : few + pair + 1] = line


def spread(me, halves, put):
    for place in range(SHARDS):
        half = halves[place * len(halves) // SHARDS]
        put(pl.multiple_of(jnp.bitwise_xor(me, place) * SUBS, SUBS), half[place % half.shape[0]])


def input_kernel(where_ref, near_ref, far_ref, fac_ref, fac_top_ref, fac_low_ref, grad_ref, grad_far_ref,
                 mine_ref, theirs_ref, left_ref, stat_ref, fac_scr, grad_scr, *, scale):
    block, me = where_ref[0], where_ref[1]
    slab, order = fac_ref.shape[1:]
    tiles = order // LANES
    own_rows = pl.ds(pl.multiple_of(block * slab, SUBS), slab)
    far_rows = pl.ds(pl.multiple_of((1 - block) * slab, SUBS), slab)
    def put(row, rows):
        stat_ref[:, pl.ds(row, SUBS), :] = rows

    spread(me, (near_ref, far_ref), put)
    fac_scr[own_rows, :] = 0.5 * fac_ref[block]
    for part, ref in enumerate((fac_top_ref, fac_low_ref)):
        first = (1 - block) * slab + part * (slab // 2)
        fac_scr[pl.ds(pl.multiple_of(first, SUBS), slab // 2), :] = 0.5 * ref[...]
    grad_scr[own_rows, :] = grad_ref[block]
    grad_scr[far_rows, :] = grad_far_ref[...]
    at = lambda n: slice(n * LANES, (n + 1) * LANES)
    index = 2
    for i in range(tiles):
        for j in range(i + 1, tiles):
            part = 0.5 * (stat_ref[index] * scale)
            fac_scr[at(i), at(j)] += part
            fac_scr[at(j), at(i)] += part.T
            index += 1
    rows, cols = places_in((LANES, LANES))
    npairs = (tiles + 1) // 2
    for pair in range(npairs):
        part = 0.5 * (stat_ref[index + pair if pair < npairs - 1 else 0] * scale)
        turned = part.T
        line = stat_ref[1, pl.ds(SUBS // 2 + pair, SHARDS, stride=SUBS), :]
        line = 0.5 * (jnp.sum(line, axis=0, keepdims=True) * scale)
        above = jnp.where(cols > rows, part, jnp.where(cols < rows, turned, line))
        fac_scr[at(2 * pair), at(2 * pair)] += above
        if pair < npairs - 1:
            fac_scr[at(2 * pair + 1), at(2 * pair + 1)] += jnp.where(cols > rows, turned, part)
    mine_ref[...] = fac_scr[own_rows, :]
    theirs_ref[...] = fac_scr[far_rows, :]
    rows = lax.broadcasted_iota(jnp.int32, (order, order), 0)
    cols = lax.broadcasted_iota(jnp.int32, (order, order), 1)
    damped = fac_scr[...] + jnp.where(rows == cols, damping, 0.0)
    squares = jnp.sum(jnp.sum(damped * damped, axis=0, keepdims=True), axis=1, keepdims=True)
    over = 1.0 / jnp.sqrt(squares)
    scaled = damped * over
    first = split(scaled)
    twice = twice_less_square(scaled, first)
    grad = grad_scr[...]
    grad = 2.0 * grad - apply3(first, grad)
    grad = 2.0 * grad - apply3(twice, grad)
    once = grad - apply3(twice, grad)
    left_ref[...] = (grad + once - apply3(twice, once)) * over


def output_kernel(where_ref, near_ref, far_ref, other_near_ref, other_far_ref, fac_ref, left_ref, _, new_ref, mine_ref, theirs_ref,
                  tile_scr, half_scr, *, scale):
    block = where_ref[0]
    few = SUBS // 2
    for n, halves in enumerate(((near_ref, far_ref), (other_near_ref, other_far_ref))):
        for place in range(SHARDS):
            shard = jnp.bitwise_xor(where_ref[1 + n], place)
            ref, at = halves[place // 8], place % 8
            tile_scr[n, pl.ds(pl.multiple_of(shard * SUBS, SUBS), SUBS), :] = ref[at, 0]
            half_scr[n, shard] = ref[at, 1]
    rows, cols = places_in((LANES, LANES))
    corners, halves = [], []
    for n in range(2):
        tile = tile_scr[n]
        corners.append(jnp.where(cols > rows, tile.T, tile))
        halves.append(jnp.concatenate([half_scr[n, s, :few, :] for s in range(SHARDS)], 0))
    first = block == 0
    upper = jnp.concatenate([jnp.where(first, halves[0], halves[1]), jnp.where(first, halves[1], halves[0])], 0)
    stats = jnp.concatenate(
        [
            jnp.concatenate([jnp.where(first, corners[0], corners[1]), upper], 1),
            jnp.concatenate([upper.T, jnp.where(first, corners[1], corners[0])], 1),
        ],
        0,
    )
    new_ref[...] = 0.5 * fac_ref[...] + 0.5 * (stats * scale)
    rows, cols = places_in(new_ref.shape)
    damped = new_ref[...] + jnp.where(rows == cols, damping, 0.0)
    squares = jnp.sum(jnp.sum(damped * damped, axis=0, keepdims=True), axis=1, keepdims=True)
    over = 1.0 / jnp.sqrt(squares)
    scaled = damped * over
    first = split(scaled)
    twice = 2.0 * scaled - mul3(first, first)
    second = split(twice)
    fourth = split(2.0 * twice - mul3(second, second))
    head = jnp.where(rows == cols, 4.0, 0.0) - 2.0 * (scaled + twice) + mul3(first, second)
    inverse = split((2.0 * head - mul3(split(head), fourth)) * over)
    slab = mine_ref.shape[0]
    theirs_ref[...] = mul3(split(left_ref[pl.ds(pl.multiple_of((1 - block) * slab, SUBS), slab), :]), inverse)
    mine_ref[...] = mul3(split(left_ref[pl.ds(pl.multiple_of(block * slab, SUBS), slab), :]), inverse)


def call(kernel, where, args, outs, scratch=(), flops=0):
    outs = [jax.ShapeDtypeStruct(shape, jnp.float32) for shape in outs]
    size = sum(array.size * array.dtype.itemsize for array in (*args, *outs))
    return pl.pallas_call(
        kernel,
        out_shape=outs,
        in_specs=[pl.BlockSpec(memory_space=pltpu.SMEM)] + [pl.BlockSpec(memory_space=pltpu.VMEM)] * len(args),
        out_specs=[pl.BlockSpec(memory_space=pltpu.VMEM)] * len(outs),
        scratch_shapes=[pltpu.VMEM(shape, jnp.float32) for shape in scratch],
        compiler_params=pltpu.CompilerParams(vmem_limit_bytes=24 << 20),
        cost_estimate=pl.CostEstimate(flops=flops, bytes_accessed=size, transcendentals=0),
    )(where, *args)


def on_chip_pairs(activations, cotangents, input_factor, output_factor, gradient, weights, momentum):
    nblocks, slab, order = input_factor.shape
    rank = output_factor.shape[0]
    group = lax.axis_index("grp")
    spot = lax.axis_index("own")
    peers = lax.axis_size("own")
    samples = activations.shape[0] * lax.axis_size("grp") * peers
    scale = 1.0 / samples
    x_bit, y_bit, z_bits = spot % 2, (spot // 2) % 2, spot // 4
    straight = x_bit * 8 + y_bit * 4 + z_bits
    crossed = y_bit * 8 + x_bit * 4 + z_bits
    me = jnp.where(group == 0, straight, crossed)
    partner = jnp.where(group == 0, crossed, straight)
    where = jnp.stack([group, me, partner]).astype(jnp.int32)
    tiles = order // LANES
    packed = [(SHARDS, 2 + tiles * (tiles - 1) // 2 + (tiles + 1) // 2 - 1, SUBS, LANES)]
    heavy = 2 * order * order * (3 * order + 12 * rank)
    fence = lax.optimization_barrier

    def swap(value):
        return lax.ppermute(value, "grp", [(0, 1), (1, 0)])

    def send(value, flips):
        pairs = [(g * peers + o, g * peers + (o ^ flips[g])) for g in range(2) for o in range(peers)]
        return lax.ppermute(value, ("grp", "own"), pairs)

    def cross(value, flips):
        pairs = [(g * peers + o, (1 - g) * peers + (o ^ flips[g])) for g in range(2) for o in range(peers)]
        return lax.ppermute(value, ("grp", "own"), pairs)

    stat_out = jnp.einsum("ti,tj->ij", cotangents, cotangents, preferred_element_type=jnp.float32)
    samples_in = (activations, stat_out)
    work = 2 * activations.shape[0] * order * order
    (theirs,) = call(lambda *refs: stats_kernel(*refs, far=True), where, samples_in, packed, (), work)
    arrived = swap(theirs[8:]), swap(theirs[:8])
    (held,) = call(lambda *refs: stats_kernel(*refs, far=False), where, samples_in, packed, (), work)
    going = held[8:] + arrived[0]
    low, going = fence((held[:8], going))
    came = send(going, (1, 2))
    kept = low + arrived[1]
    fac_rows = lax.dynamic_index_in_dim(input_factor, 1 - group, 0, False)
    grad_rows = lax.dynamic_index_in_dim(gradient, 1 - group, 0, False)
    fac_far = swap(fac_rows[: slab // 2]), swap(fac_rows[slab // 2 :])
    grad_far = swap(grad_rows)
    came, fac_far, grad_far = fence((came, fac_far, grad_far))
    came = send(kept[4:] + came[4:], (2, 1)), kept[:4] + came[:4]
    kept = came[0] + came[1]
    ways = (3, 2, 1)
    pieces = {d: send(kept[d : d + 1], (4 * d, 4 * d)) for d in ways}
    kept = kept[:1] + pieces[3] + pieces[2] + pieces[1]
    pieces = {d: send(kept, (4 * d, 4 * d)) for d in ways}
    pace = swap(pieces[3][:, :1])
    kept = jnp.concatenate([kept, pieces[1], pieces[2], pieces[3]], 0)
    kept, pace = fence((kept, pace))
    near = jnp.concatenate([kept, send(kept, (2, 1))], 0)
    far = send(near, (1, 2))
    share = near[:, :2]
    beside = swap(share)
    across = cross(share, (1, 2))
    far, beside, across = fence((far, beside, across))
    mine, theirs, left = call(
        lambda *refs: input_kernel(*refs, scale=scale),
        where,
        (near, far, input_factor, *fac_far, gradient, grad_far),
        [(slab, order), (slab, order), (order, rank)],
        [(packed[0][1], LANES, LANES), (order, order), (order, rank)],
        heavy,
    )
    new_output, update, update_far = call(
        lambda *refs: output_kernel(*refs, scale=scale),
        where,
        (near, far, beside, across, output_factor, left, pace),
        [(rank, rank), (slab, rank), (slab, rank)],
        [(2, LANES, LANES), (2, SHARDS, SUBS, LANES)],
        24 * rank * rank * rank + 6 * order * rank * rank,
    )
    rows_far = swap(theirs)
    update_far = swap(update_far)
    own_block = lax.broadcasted_iota(jnp.int32, (nblocks, 1, 1), 0) == group
    new_input = jnp.where(own_block, mine[None], rows_far[None])
    update_far, _ = fence((update_far, new_input))
    new_momentum = mom_decay * momentum + jnp.where(own_block, update[None], update_far[None])
    new_weights = weights - step_size * new_momentum
    return (new_weights, new_momentum, new_input, new_output)


def solution(mesh):
    placed = (
        P(("grp", "own"), None),
        P(("grp", "own"), None),
        P(None, "grp", None),
        P(),
        P(None, "grp", None),
        P(None, "grp", None),
        P(None, "grp", None),
    )

    def on_device(*args):
        nblocks, slab, order = args[2].shape
        rank = args[3].shape[0]
        fits = nblocks == 2 and order % LANES == 0 and slab % (2 * SUBS) == 0 and rank == 2 * LANES and order // LANES in (1, 3, 5, 7)
        paired = mesh.shape["grp"] == 2 and mesh.shape["own"] == SHARDS
        return (on_chip_pairs if fits and paired else any_mesh)(*args)

    return jax.shard_map(
        on_device,
        mesh=mesh,
        in_specs=placed,
        out_specs=(P(None, "grp", None), P(None, "grp", None), P(None, "grp", None), P()),
        check_vma=False,
    )
```

```python
import jax
import jax.numpy as jnp
from jax import lax
from jax.experimental import pallas as pl
from jax.experimental.pallas import tpu as pltpu
from jax.sharding import PartitionSpec as P

ITERS = 3


damping = 0.1
mom_decay = 0.9
step_size = 0.5

LANES = 128
SUBS = 8
SHARDS = 16


def newton_start(damped, ident):
    squares = jnp.sum(damped * damped, axis=(-2, -1), keepdims=True)
    bound = jnp.sqrt(squares)
    return 2.0 / bound * ident - damped / (bound * bound)


def step_rows(damped_rows, own_rows, full_iterate):
    product = jnp.matmul(damped_rows, full_iterate, precision=lax.Precision.HIGHEST)
    return 2.0 * own_rows - jnp.matmul(product, full_iterate, precision=lax.Precision.HIGHEST)


def any_mesh(activations, cotangents, input_factor, output_factor, gradient, weights, momentum):
    nblocks, slab, order = input_factor.shape
    rank = output_factor.shape[0]
    tokens = activations.shape[0]
    groups = lax.axis_size("grp")
    samples = tokens * groups * lax.axis_size("own")
    first_row = lax.axis_index("grp") * slab
    split_in = activations.reshape(tokens, nblocks, order)
    stat_in = jnp.einsum("tki,tkj->kij", split_in, split_in, preferred_element_type=jnp.float32)
    stat_out = jnp.einsum("ti,tj->ij", cotangents, cotangents, preferred_element_type=jnp.float32)
    total_in, total_out = lax.psum((stat_in, stat_out), ("grp", "own"))
    share_in = lax.dynamic_slice_in_dim(total_in, first_row, slab, 1)
    new_input = 0.5 * input_factor + 0.5 * (share_in / samples)
    new_output = 0.5 * output_factor + 0.5 * (total_out / samples)
    rows_in = lax.broadcasted_iota(jnp.int32, (slab, order), 0) + first_row
    cols_in = lax.broadcasted_iota(jnp.int32, (slab, order), 1)
    ident_rows = (rows_in == cols_in).astype(jnp.float32)
    ident_out = jnp.eye(rank, dtype=jnp.float32)
    damped_in = new_input + damping * ident_rows
    damped_out = new_output + damping * ident_out
    squares = lax.psum(jnp.sum(damped_in * damped_in, axis=(1, 2), keepdims=True), "grp")
    bound = jnp.sqrt(squares)
    iterate_in = 2.0 / bound * ident_rows - damped_in / (bound * bound)
    start_out = newton_start(damped_out, ident_out)
    out_rows = rank // groups
    first_out = lax.axis_index("grp") * out_rows
    damped_rows = lax.dynamic_slice_in_dim(damped_out, first_out, out_rows, 0)
    iterate_out = lax.dynamic_slice_in_dim(start_out, first_out, out_rows, 0)
    for iteration in range(ITERS - 1):
        full_in, full_out = (
            lax.all_gather(iterate_in, "grp", axis=1, tiled=True),
            lax.all_gather(iterate_out, "grp", axis=0, tiled=True),
        )
        iterate_in = step_rows(damped_in, iterate_in, full_in)
        iterate_out = step_rows(damped_rows, iterate_out, full_out)
    inverse_out = lax.all_gather(iterate_out, "grp", axis=0, tiled=True)
    precond = jnp.einsum(
        "kij,kjr->kir",
        iterate_in,
        lax.all_gather(gradient, "grp", axis=1, tiled=True),
        precision=lax.Precision.HIGHEST,
    )
    update = jnp.einsum("kir,rs->kis", precond, inverse_out, precision=lax.Precision.HIGHEST)
    new_momentum = mom_decay * momentum + update
    new_weights = weights - step_size * new_momentum
    return (new_weights, new_momentum, new_input, new_output)


def split(value):
    high = value.astype(jnp.bfloat16)
    low = (value - high.astype(jnp.float32)).astype(jnp.bfloat16)
    return high, low


def mul(a, b):
    return jnp.dot(a, b, preferred_element_type=jnp.float32)


def mul3(a, b):
    return mul(a[0], b[0]) + (mul(a[0], b[1]) + mul(a[1], b[0]))


def long3(a, b):
    return mul(jnp.concatenate([a[0], a[1], a[0]], 1), jnp.concatenate([b[0], b[0], b[1]], 0))


def apply3(a, b):
    b = split(b)
    half = a[0].shape[0] // 2
    return jnp.concatenate([long3([v[:half] for v in a], b), long3([v[half:] for v in a], b)], 0)


def twice_less_square(value, halves):
    order = value.shape[0]
    ends = list(range(order, 0, -2 * LANES))[::-1]
    strips = []
    for end in ends:
        cols = slice(max(end - 2 * LANES, 0), end)
        square = long3([v[:end] for v in halves], [v[:, cols] for v in halves])
        strips.append(split(2.0 * value[:end, cols] - square))
    parts = []
    for part in range(2):
        rows = []
        for n, end in enumerate(ends):
            top = ends[n - 1] if n else 0
            left = [strips[n][part][:top].T] if n else []
            right = [strips[m][part][top:end] for m in range(n, len(ends))]
            rows.append(jnp.concatenate(left + right, 1))
        parts.append(jnp.concatenate(rows, 0))
    return parts


def tile_pairs(tiles):
    return [(i, j) for i in range(tiles) for j in range(i, tiles)]


def places_in(shape):
    rows = lax.broadcasted_iota(jnp.int32, shape, 0)
    cols = lax.broadcasted_iota(jnp.int32, shape, 1)
    return rows, cols


def stats_kernel(where_ref, act_ref, out_ref, packed_ref, *, far):
    block = 1 - where_ref[0] if far else where_ref[0]
    me = where_ref[2] if far else where_ref[1]
    order = act_ref.shape[1] // 2
    tiles = order // LANES
    places = [jnp.bitwise_xor(me, s) for s in range(SHARDS)]

    def put(index, tile):
        for s in range(SHARDS):
            packed_ref[places[s], index] = tile[s * SUBS : (s + 1) * SUBS]

    index = 2
    act = act_ref[:, pl.ds(pl.multiple_of(block * order, LANES), order)]
    turned = act.T
    diagonal = []
    for i in range(tiles):
        strip = mul(turned[i * LANES : (i + 1) * LANES], act[:, i * LANES :])
        diagonal.append(strip[:, :LANES])
        for j in range(1, tiles - i):
            put(index, strip[:, j * LANES : (j + 1) * LANES])
            index += 1
    here = pl.ds(pl.multiple_of(block * LANES, LANES), LANES)
    diagonal.append(out_ref[here, here])
    half = LANES // 2
    upper = out_ref[pl.ds(pl.multiple_of(block * half, SUBS), half), LANES:]
    rows, cols = places_in((LANES, LANES))
    npairs = len(diagonal) // 2
    lines = []
    for pair in range(npairs):
        above, below = diagonal[2 * pair], diagonal[2 * pair + 1]
        put(index + pair if pair < npairs - 1 else 0, jnp.where(cols > rows, above, below))
        lines.append(jnp.sum(jnp.where(cols == rows, above, 0.0).reshape(SHARDS, SUBS, LANES), axis=1))
    few = SUBS // 2
    for s in range(SHARDS):
        packed_ref[places[s], 1, :few] = upper[s * few : (s + 1) * few]
        for pair in range(few):
            line = lines[pair][s : s + 1] if pair < npairs else jnp.zeros((1, LANES), jnp.float32)
            packed_ref[places[s], 1, few + pair : few + pair + 1] = line


def spread(me, halves, put):
    for place in range(SHARDS):
        half = halves[place * len(halves) // SHARDS]
        put(pl.multiple_of(jnp.bitwise_xor(me, place) * SUBS, SUBS), half[place % half.shape[0]])


def input_kernel(where_ref, near_ref, far_ref, fac_ref, fac_top_ref, fac_low_ref, grad_ref, grad_far_ref,
                 mine_ref, theirs_ref, left_ref, stat_ref, fac_scr, grad_scr, *, scale):
    block, me = where_ref[0], where_ref[1]
    slab, order = fac_ref.shape[1:]
    tiles = order // LANES
    own_rows = pl.ds(pl.multiple_of(block * slab, SUBS), slab)
    far_rows = pl.ds(pl.multiple_of((1 - block) * slab, SUBS), slab)
    def put(row, rows):
        stat_ref[:, pl.ds(row, SUBS), :] = rows

    spread(me, (near_ref, far_ref), put)
    fac_scr[own_rows, :] = 0.5 * fac_ref[block]
    for part, ref in enumerate((fac_top_ref, fac_low_ref)):
        first = (1 - block) * slab + part * (slab // 2)
        fac_scr[pl.ds(pl.multiple_of(first, SUBS), slab // 2), :] = 0.5 * ref[...]
    grad_scr[own_rows, :] = grad_ref[block]
    grad_scr[far_rows, :] = grad_far_ref[...]
    at = lambda n: slice(n * LANES, (n + 1) * LANES)
    index = 2
    for i in range(tiles):
        for j in range(i + 1, tiles):
            part = 0.5 * (stat_ref[index] * scale)
            fac_scr[at(i), at(j)] += part
            fac_scr[at(j), at(i)] += part.T
            index += 1
    rows, cols = places_in((LANES, LANES))
    npairs = (tiles + 1) // 2
    for pair in range(npairs):
        part = 0.5 * (stat_ref[index + pair if pair < npairs - 1 else 0] * scale)
        turned = part.T
        line = stat_ref[1, pl.ds(SUBS // 2 + pair, SHARDS, stride=SUBS), :]
        line = 0.5 * (jnp.sum(line, axis=0, keepdims=True) * scale)
        above = jnp.where(cols > rows, part, jnp.where(cols < rows, turned, line))
        fac_scr[at(2 * pair), at(2 * pair)] += above
        if pair < npairs - 1:
            fac_scr[at(2 * pair + 1), at(2 * pair + 1)] += jnp.where(cols > rows, turned, part)
    mine_ref[...] = fac_scr[own_rows, :]
    theirs_ref[...] = fac_scr[far_rows, :]
    rows = lax.broadcasted_iota(jnp.int32, (order, order), 0)
    cols = lax.broadcasted_iota(jnp.int32, (order, order), 1)
    damped = fac_scr[...] + jnp.where(rows == cols, damping, 0.0)
    squares = jnp.sum(jnp.sum(damped * damped, axis=0, keepdims=True), axis=1, keepdims=True)
    over = 1.0 / jnp.sqrt(squares)
    scaled = damped * over
    first = split(scaled)
    twice = twice_less_square(scaled, first)
    grad = grad_scr[...]
    grad = 2.0 * grad - apply3(first, grad)
    grad = 2.0 * grad - apply3(twice, grad)
    once = grad - apply3(twice, grad)
    left_ref[...] = (grad + once - apply3(twice, once)) * over


def output_kernel(where_ref, near_ref, far_ref, other_near_ref, other_far_ref, fac_ref, left_ref, _pace, _early, new_ref, mine_ref, theirs_ref,
                  tile_scr, half_scr, *, scale):
    block = where_ref[0]
    few = SUBS // 2
    for n, halves in enumerate(((near_ref, far_ref), (other_near_ref, other_far_ref))):
        for place in range(SHARDS):
            shard = jnp.bitwise_xor(where_ref[1 + n], place)
            ref, at = halves[place // 8], place % 8
            tile_scr[n, pl.ds(pl.multiple_of(shard * SUBS, SUBS), SUBS), :] = ref[at, 0]
            half_scr[n, shard] = ref[at, 1]
    rows, cols = places_in((LANES, LANES))
    corners, halves = [], []
    for n in range(2):
        tile = tile_scr[n]
        corners.append(jnp.where(cols > rows, tile.T, tile))
        halves.append(jnp.concatenate([half_scr[n, s, :few, :] for s in range(SHARDS)], 0))
    first = block == 0
    upper = jnp.concatenate([jnp.where(first, halves[0], halves[1]), jnp.where(first, halves[1], halves[0])], 0)
    stats = jnp.concatenate(
        [
            jnp.concatenate([jnp.where(first, corners[0], corners[1]), upper], 1),
            jnp.concatenate([upper.T, jnp.where(first, corners[1], corners[0])], 1),
        ],
        0,
    )
    new_ref[...] = 0.5 * fac_ref[...] + 0.5 * (stats * scale)
    rows, cols = places_in(new_ref.shape)
    damped = new_ref[...] + jnp.where(rows == cols, damping, 0.0)
    squares = jnp.sum(jnp.sum(damped * damped, axis=0, keepdims=True), axis=1, keepdims=True)
    over = 1.0 / jnp.sqrt(squares)
    scaled = damped * over
    first = split(scaled)
    twice = 2.0 * scaled - mul3(first, first)
    second = split(twice)
    fourth = split(2.0 * twice - mul3(second, second))
    head = jnp.where(rows == cols, 4.0, 0.0) - 2.0 * (scaled + twice) + mul3(first, second)
    inverse = split((2.0 * head - mul3(split(head), fourth)) * over)
    slab = mine_ref.shape[0]
    theirs_ref[...] = mul3(split(left_ref[pl.ds(pl.multiple_of((1 - block) * slab, SUBS), slab), :]), inverse)
    mine_ref[...] = mul3(split(left_ref[pl.ds(pl.multiple_of(block * slab, SUBS), slab), :]), inverse)


def call(kernel, where, args, outs, scratch=(), flops=0):
    outs = [jax.ShapeDtypeStruct(shape, jnp.float32) for shape in outs]
    size = sum(array.size * array.dtype.itemsize for array in (*args, *outs))
    return pl.pallas_call(
        kernel,
        out_shape=outs,
        in_specs=[pl.BlockSpec(memory_space=pltpu.SMEM)] + [pl.BlockSpec(memory_space=pltpu.VMEM)] * len(args),
        out_specs=[pl.BlockSpec(memory_space=pltpu.VMEM)] * len(outs),
        scratch_shapes=[pltpu.VMEM(shape, jnp.float32) for shape in scratch],
        compiler_params=pltpu.CompilerParams(vmem_limit_bytes=24 << 20),
        cost_estimate=pl.CostEstimate(flops=flops, bytes_accessed=size, transcendentals=0),
    )(where, *args)


def on_chip_pairs(activations, cotangents, input_factor, output_factor, gradient, weights, momentum):
    nblocks, slab, order = input_factor.shape
    rank = output_factor.shape[0]
    group = lax.axis_index("grp")
    spot = lax.axis_index("own")
    peers = lax.axis_size("own")
    samples = activations.shape[0] * lax.axis_size("grp") * peers
    scale = 1.0 / samples
    x_bit, y_bit, z_bits = spot % 2, (spot // 2) % 2, spot // 4
    straight = x_bit * 8 + y_bit * 4 + z_bits
    crossed = y_bit * 8 + x_bit * 4 + z_bits
    me = jnp.where(group == 0, straight, crossed)
    partner = jnp.where(group == 0, crossed, straight)
    where = jnp.stack([group, me, partner]).astype(jnp.int32)
    tiles = order // LANES
    packed = [(SHARDS, 2 + tiles * (tiles - 1) // 2 + (tiles + 1) // 2 - 1, SUBS, LANES)]
    heavy = 2 * order * order * (3 * order + 12 * rank)
    fence = lax.optimization_barrier

    def swap(value):
        return lax.ppermute(value, "grp", [(0, 1), (1, 0)])

    def send(value, flips):
        pairs = [(g * peers + o, g * peers + (o ^ flips[g])) for g in range(2) for o in range(peers)]
        return lax.ppermute(value, ("grp", "own"), pairs)

    def cross(value, flips):
        pairs = [(g * peers + o, (1 - g) * peers + (o ^ flips[g])) for g in range(2) for o in range(peers)]
        return lax.ppermute(value, ("grp", "own"), pairs)

    stat_out = jnp.einsum("ti,tj->ij", cotangents, cotangents, preferred_element_type=jnp.float32)
    samples_in = (activations, stat_out)
    work = 2 * activations.shape[0] * order * order
    (theirs,) = call(lambda *refs: stats_kernel(*refs, far=True), where, samples_in, packed, (), work)
    arrived = swap(theirs[8:]), swap(theirs[:8])
    (held,) = call(lambda *refs: stats_kernel(*refs, far=False), where, samples_in, packed, (), work)
    going = held[8:] + arrived[0]
    low, going = fence((held[:8], going))
    came = send(going, (1, 2))
    kept = low + arrived[1]
    fac_rows = lax.dynamic_index_in_dim(input_factor, 1 - group, 0, False)
    grad_rows = lax.dynamic_index_in_dim(gradient, 1 - group, 0, False)
    fac_far = swap(fac_rows[: slab // 2]), swap(fac_rows[slab // 2 :])
    grad_far = swap(grad_rows)
    came, fac_far, grad_far = fence((came, fac_far, grad_far))
    early = swap(fac_far[0][:SUBS, :LANES])
    came, early = fence((came, early))
    came = send(kept[4:] + came[4:], (2, 1)), kept[:4] + came[:4]
    kept = came[0] + came[1]
    ways = (3, 2, 1)
    pieces = {d: send(kept[d : d + 1], (4 * d, 4 * d)) for d in ways}
    kept = kept[:1] + pieces[3] + pieces[2] + pieces[1]
    pieces = {d: send(kept, (4 * d, 4 * d)) for d in ways}
    pace = swap(pieces[3][:, :1])
    kept = jnp.concatenate([kept, pieces[1], pieces[2], pieces[3]], 0)
    kept, pace = fence((kept, pace))
    near = jnp.concatenate([kept, send(kept, (2, 1))], 0)
    far = send(near, (1, 2))
    share = near[:, :2]
    beside = swap(share)
    across = cross(share, (1, 2))
    far, beside, across = fence((far, beside, across))
    mine, theirs, left = call(
        lambda *refs: input_kernel(*refs, scale=scale),
        where,
        (near, far, input_factor, *fac_far, gradient, grad_far),
        [(slab, order), (slab, order), (order, rank)],
        [(packed[0][1], LANES, LANES), (order, order), (order, rank)],
        heavy,
    )
    new_output, update, update_far = call(
        lambda *refs: output_kernel(*refs, scale=scale),
        where,
        (near, far, beside, across, output_factor, left, pace, early),
        [(rank, rank), (slab, rank), (slab, rank)],
        [(2, LANES, LANES), (2, SHARDS, SUBS, LANES)],
        24 * rank * rank * rank + 6 * order * rank * rank,
    )
    rows_far = swap(theirs)
    update_far = swap(update_far)
    own_block = lax.broadcasted_iota(jnp.int32, (nblocks, 1, 1), 0) == group
    new_input = jnp.where(own_block, mine[None], rows_far[None])
    update_far, _ = fence((update_far, new_input))
    new_momentum = mom_decay * momentum + jnp.where(own_block, update[None], update_far[None])
    new_weights = weights - step_size * new_momentum
    return (new_weights, new_momentum, new_input, new_output)


def solution(mesh):
    placed = (
        P(("grp", "own"), None),
        P(("grp", "own"), None),
        P(None, "grp", None),
        P(),
        P(None, "grp", None),
        P(None, "grp", None),
        P(None, "grp", None),
    )

    def on_device(*args):
        nblocks, slab, order = args[2].shape
        rank = args[3].shape[0]
        fits = nblocks == 2 and order % LANES == 0 and slab % (2 * SUBS) == 0 and rank == 2 * LANES and order // LANES in (1, 3, 5, 7)
        paired = mesh.shape["grp"] == 2 and mesh.shape["own"] == SHARDS
        return (on_chip_pairs if fits and paired else any_mesh)(*args)

    return jax.shard_map(
        on_device,
        mesh=mesh,
        in_specs=placed,
        out_specs=(P(None, "grp", None), P(None, "grp", None), P(None, "grp", None), P()),
        check_vma=False,
    )
```
